128 devices in a mesh: facet: 8 (over z, core), vis: 16 (over y, x).
Axes of the slice: x: 4, y: 4, z: 4, core: 2. Of those that a mesh axis runs over, the one named last changes fastest.
Arguments:
- vis_obs: float32 [16384, 2, 4, 1024], P(('facet', 'vis')), may hold values from -6 to 6
- uv_coords: float32 [16384, 2, 1024], P(('facet', 'vis')), may hold values from -16 to 16
- vis_weight: float32 [16384, 1024], P(('facet', 'vis')), may hold values from 0.5 to 900, as said below
- block_group: int32 [16384, 1], P(('facet', 'vis')), may hold values from 0 to 127; in each aligned block of 128 rows (0 to 127, 128 to 255, ...) at most 2 rows name the same one
- tile_slot: int32 [16384], P(('facet', 'vis')), may hold values from 0 to 63
- w_plane: int32 [16384], P(('facet', 'vis')), may hold values from 0 to 31
- model_tiles: bfloat16 [8192, 2, 32, 128], P(('facet', 'vis')), may hold values from -6 to 6
- w_kernels: bfloat16 [32, 2, 32, 32], replicated, may hold values from -0.75 to 0.75
Outputs:
- residual_vis: float32 [16384, 2, 4, 1024], P(('facet', 'vis'))
- residual_tiles: float32 [8192, 2, 32, 128], P(('facet', 'vis'))
The draws below stay inside these ranges and needn't reach their ends.
Inputs may be any that keep to these rules, and one draw needn't show every extreme that they name: `block_group`: in the 128 rows of one device (aligned blocks of 128 rows) no group is named by more than 2 rows, a bound that some block reaches. `vis_weight`: Positive.
All inputs are finite; a program needn't handle non-finite values.
Results may differ from the reference program's by a relative error of at most 0.0045.
Values may be sent and summed in bfloat16 or wider, within the bound.
A program may use at most 128 MiB of HBM per device.

```python
import math
import jax
import jax.numpy as jnp
import numpy as np
from jax import lax

S = 32
P_SIZE = 4
NVIS = 1024
WPLANES = 32
BLK_DEV = 128
TILE_DEV = 64
GROUPS = 128
CAP = 2
NBLK = 16384
NTILES = 8192


def draw_vis_weight(key, part):
    key_rows = jax.random.fold_in(key, 11)
    key_columns = jax.random.fold_in(key, 12)
    key_entries = jax.random.fold_in(key, 13)
    position = jnp.arange(NBLK, dtype=jnp.float32)[:, None] / max(NBLK - 1, 1)
    row_scale = jnp.exp(jax.random.uniform(key_rows, (NBLK, 1), jnp.float32, 0.0, math.log(10.0)))
    column_scale = jnp.exp(jax.random.uniform(key_columns, (1, NVIS), jnp.float32, 0.0, math.log(10.0)))
    fine_scale = jax.random.uniform(key_entries, (NBLK, NVIS), jnp.float32, 0.5, 1.0)
    ramp_scale = 1.0 + 2.0 * position
    return (ramp_scale * row_scale * column_scale * fine_scale).astype(jnp.float32)


def touch_ends(array, rng, low, largest):
    index_at = [jax.random.randint(jax.random.fold_in(rng, axis), (), 0, length) for axis, length in enumerate(array.shape)]
    widest = array.shape.index(max(array.shape))
    beside = index_at[:widest] + [(index_at[widest] + 1) % array.shape[widest]] + index_at[widest + 1:]
    return array.at[tuple(index_at)].set(low).at[tuple(beside)].set(largest)


def level_of(key, extent, split, low, largest):
    gain, own = 1.0, jax.random.fold_in(key, 6)
    for dim, blocks in split:
        steps = jnp.exp(jax.random.uniform(jax.random.fold_in(own, dim), (blocks,), jnp.float32, low / len(split), largest / len(split)))
        gain = gain * jnp.repeat(steps, extent[dim] // blocks).reshape([-1 if axis == dim else 1 for axis in range(len(extent))])
    return gain


def deal_out(own_key, own, number, rows, number_of, top, bound, slope):
    ranking = jax.random.permutation(own_key, number_of)
    packed, ordinary = load_shares(number_of, rows * top, bound, slope, True), load_shares(number_of, rows * top, bound, slope, False)
    places = jnp.arange(number_of)

    def named(lengths, turn):
        used = int((lengths > 0).sum())
        fixed = max(1, used // 4)
        shifted = fixed + (places - fixed + turn * (used - fixed)) % max(1, number_of - fixed)
        return jnp.zeros((number_of,), jnp.int32).at[ranking[jnp.where(places < fixed, places, shifted)]].set(jnp.asarray(lengths, jnp.int32))

    lengths = jnp.where(number % 4 == 0, named(packed, number // 4), named(ordinary, number - number // 4 - 1))
    mixed = jax.random.permutation(jax.random.fold_in(own, 3), number_of)
    source_of, sink = mixed[0:number_of // 2 * 2:2], mixed[1:number_of // 2 * 2:2]
    slack = jnp.minimum(lengths[source_of] - 1, bound - lengths[sink]) // 2
    slack = jnp.where((source_of == ranking[0]) | (sink == ranking[0]) | (lengths[sink] == 0), 0, jnp.maximum(slack, 0))
    shifted = jax.random.randint(jax.random.fold_in(own, 4), (number_of // 2,), 0, 1 << 20) % (slack + 1)
    lengths = lengths.at[source_of].add(-shifted).at[sink].add(shifted)
    items = jnp.searchsorted(jnp.cumsum(lengths), jnp.arange(rows * top), side="right").astype(jnp.int32)
    table = items.reshape(top, rows).T
    table = table[jax.random.permutation(jax.random.fold_in(own, 1), rows)]
    turn = jax.random.randint(jax.random.fold_in(own, 2), (rows, 1), 0, top)
    return jnp.take_along_axis(table, (jnp.arange(top)[None, :] + turn) % top, axis=1)


def load_shares(amount, total, bound, slope, full):
    weights = [(1 << 20) // math.isqrt(grade ** slope) + 1 for grade in range(1, amount + 1)]
    largest = bound if full else min(bound, max(-(-total // amount), total * weights[0] // sum(weights)))
    least = 1 if total - largest >= amount - 1 else 0
    counts, spare = [largest] + [least] * (amount - 1), total - largest - least * (amount - 1)
    while spare > 0:
        candidates = [i for i in range(1, amount) if counts[i] < largest] or [i for i in range(1, amount) if counts[i] < bound]
        pool, budget = sum([weights[i] for i in candidates]), spare
        for i in candidates:
            more = min(bound - counts[i], max(1, budget * weights[i] // pool), spare)
            counts[i] = counts[i] + more
            spare = spare - more
    return np.array(counts)


def noise(own_key, extent, width, limit, pieces=(), kind=jnp.bfloat16):
    entries = jax.random.normal(own_key, extent, jnp.float32) * width
    if len(pieces) > 0:
        entries = level_of(own_key, extent, pieces, -0.22, 0.18) * entries
    return jnp.clip(entries, min=-limit, max=limit).astype(kind)


def setup_inputs(seed: int = 0) -> dict:
    key_of = jax.random.split(jax.random.key(seed), 9)
    vis_obs = noise(key_of[0], (NBLK, 2, P_SIZE, NVIS), 1.0, 6.0, ((0, 128),), jnp.float32)
    uv_coords = jnp.clip(jax.random.uniform(key_of[1], (NBLK, 2, NVIS), jnp.float32, -16.0, 16.0) * level_of(key_of[1], (NBLK, 2, NVIS), ((0, 128),), -0.4, 0.0), -16.0, 16.0)
    vis_weight = draw_vis_weight(jax.random.fold_in(key_of[8], 71), 0)
    block_group_keys = jax.random.split(jax.random.fold_in(key_of[3], 1), NBLK // BLK_DEV)
    block_group_turns = jax.random.permutation(jax.random.fold_in(key_of[3], 3), NBLK // BLK_DEV)
    block_group = jax.vmap(lambda own, number: deal_out(jax.random.fold_in(key_of[3], 2), own, number, BLK_DEV, GROUPS, 1, CAP, 2))(block_group_keys, block_group_turns).reshape((NBLK, 1))
    tile_slot = touch_ends(jax.random.randint(key_of[4], (NBLK,), 0, TILE_DEV), jax.random.fold_in(key_of[4], 1), 0, TILE_DEV - 1).astype(jnp.int32)
    w_plane = touch_ends(jax.random.randint(key_of[5], (NBLK,), 0, WPLANES), jax.random.fold_in(key_of[5], 1), 0, WPLANES - 1).astype(jnp.int32)
    model_tiles = noise(key_of[6], (NTILES, 2, S, P_SIZE * S), 1.0, 6.0, ((0, 128),))
    w_kernels = noise(key_of[7], (WPLANES, 2, S, S), (2 * S) ** -0.5, 0.75)
    return {"vis_obs": vis_obs, "uv_coords": uv_coords, "vis_weight": vis_weight, "block_group": block_group, "tile_slot": tile_slot, "w_plane": w_plane, "model_tiles": model_tiles, "w_kernels": w_kernels}


def rounded(operand):
    return lax.optimization_barrier(operand.astype(jnp.bfloat16))


def complex_product(form_text, left_side, right_side):
    left_side = left_side.astype(jnp.float32)
    right_side = right_side.astype(jnp.float32)
    real_part = jnp.einsum(form_text, left_side[:, 0], right_side[:, 0]) - jnp.einsum(form_text, left_side[:, 1], right_side[:, 1])
    imag_part = jnp.einsum(form_text, left_side[:, 0], right_side[:, 1]) + jnp.einsum(form_text, left_side[:, 1], right_side[:, 0])
    return jnp.stack((real_part, imag_part), axis=1)


def conjugate(operand):
    return jnp.stack((operand[:, 0], -operand[:, 1]), axis=1)


def phasors(coordinates, sub_width):
    offsets = (jnp.arange(sub_width) - sub_width // 2).astype(jnp.float32) * (-2.0 * math.pi / sub_width)
    angles = coordinates[:, :, None, :] * offsets[None, None, :, None]
    return jnp.cos(angles), jnp.sin(angles)


def degrid_grid(tile_rows, kernels, coordinates, observed, weights):
    block_count = tile_rows.shape[0]
    sub_width = tile_rows.shape[2]
    span_width = tile_rows.shape[3]
    pol_count = span_width // sub_width
    vis_count = coordinates.shape[-1]
    left_prod = rounded(complex_product("nij,njq->niq", kernels, tile_rows))
    left_prod = left_prod.reshape(block_count, 2, sub_width, pol_count, sub_width)
    kerneled = rounded(complex_product("nlpm,nkm->nlpk", left_prod, kernels).reshape(block_count, 2, sub_width, span_width))
    cosine, sine_part = phasors(coordinates, sub_width)
    along_u = rounded(jnp.stack((cosine[:, 0], sine_part[:, 0]), axis=1))
    phase_real = cosine[:, 1][:, None]
    phase_imag = sine_part[:, 1][:, None]
    spread = complex_product("nlq,nlk->nqk", kerneled, along_u).reshape(block_count, 2, pol_count, sub_width, vis_count)
    predicted_real = jnp.sum(spread[:, 0] * phase_real - spread[:, 1] * phase_imag, axis=2) / sub_width
    predicted_imag = jnp.sum(spread[:, 0] * phase_imag + spread[:, 1] * phase_real, axis=2) / sub_width
    residual = observed - jnp.stack((predicted_real, predicted_imag), axis=1)
    factor = (weights / sub_width)[:, None, None, :]
    residual_real = residual[:, 0][:, :, None, :]
    residual_imag = residual[:, 1][:, :, None, :]
    weighted_real = (residual_real * phase_real + residual_imag * phase_imag) * factor
    weighted_imag = (residual_imag * phase_real - residual_real * phase_imag) * factor
    weighted = rounded(jnp.stack((weighted_real, weighted_imag), axis=1).reshape(block_count, 2, span_width, vis_count))
    gridded = rounded(complex_product("nlk,nqk->nlq", conjugate(along_u), weighted))
    back_prod = rounded(complex_product("nji,njq->niq", conjugate(kernels), gridded))
    back_prod = back_prod.reshape(block_count, 2, sub_width, pol_count, sub_width)
    contribution = complex_product("nlpm,nmk->nlpk", back_prod, conjugate(kernels)).reshape(block_count, 2, sub_width, span_width)
    return residual, contribution


def reference(vis_obs, uv_coords, vis_weight, block_group, tile_slot, w_plane, model_tiles, w_kernels):
    block_count = vis_obs.shape[0]
    batch_size = math.gcd(block_count, 64)
    tile_index = (block_group[:, 0] * TILE_DEV + tile_slot).astype(jnp.int32)

    def split_blocks(operand):
        return operand.reshape((block_count // batch_size, batch_size) + operand.shape[1:])

    def process(inputs):
        index_part, plane_part, coord_part, observed, weights = inputs
        tile_rows = jnp.take(model_tiles, index_part, axis=0)
        kernels = jnp.take(w_kernels, plane_part, axis=0)
        return degrid_grid(tile_rows, kernels, coord_part, observed, weights)

    residual, contribution = lax.map(process, (split_blocks(tile_index), split_blocks(w_plane), split_blocks(uv_coords), split_blocks(vis_obs), split_blocks(vis_weight)))
    residual = residual.reshape(vis_obs.shape)
    contribution = contribution.reshape((block_count,) + model_tiles.shape[1:])
    summed = jax.ops.segment_sum(contribution, tile_index, num_segments=model_tiles.shape[0])
    weight_sum = jnp.sum(vis_weight)
    scaling = (block_count * vis_obs.shape[-1]) / weight_sum
    return residual, summed * scaling
```

```python
import jax
import jax.numpy as jnp
import numpy as np
from jax import lax
from jax.experimental import pallas as pl
from jax.experimental.pallas import tpu as pltpu
from jax.sharding import PartitionSpec as P

AXES = ("facet", "vis")
CAP = 2

BF = jnp.bfloat16
F32 = jnp.float32
STEP = 8
CHUNK = 256


def even_fit(func, terms):
    nodes = np.cos(np.pi * (np.arange(200) + 0.5) / 200) * 0.25
    squares = (nodes + 0.25) / 2
    powers = squares[:, None] ** np.arange(terms)[None, :]
    scale = powers.max(axis=0)
    solved = np.linalg.lstsq(powers / scale, func(np.sqrt(squares)), rcond=None)[0]
    return [float(value) for value in solved / scale]


COS_TERMS = even_fit(lambda t: np.cos(np.pi * t), 7)
SIN_TERMS = even_fit(lambda t: np.sin(np.pi * t) / t, 6)


def half_turn(t):
    square = t * t
    cosine = jnp.full_like(t, COS_TERMS[-1])
    for term in COS_TERMS[-2::-1]:
        cosine = cosine * square + term
    sine = jnp.full_like(t, SIN_TERMS[-1])
    for term in SIN_TERMS[-2::-1]:
        sine = sine * square + term
    return cosine, sine * t


def nt_dot(left, right):
    return lax.dot_general(left, right, (((1,), (1,)), ((), ())), preferred_element_type=F32)


def tn_dot(left, right):
    return lax.dot_general(left, right, (((0,), (0,)), ((), ())), preferred_element_type=F32)


def nn_dot(left, right):
    return jnp.dot(left, right, preferred_element_type=F32)


def lay(table, row, pitch, value):
    for t in range(value.shape[1] // 128):
        table[t, pl.ds(row, STEP, stride=pitch), :] = value[:, 128 * t:128 * t + 128]


def rows_of(table, first, count, start, out_rows):
    pieces = [
        jnp.broadcast_to(table[start // 128 + t, first:first + count, :], (out_rows, 128))
        for t in range(CHUNK // 128)
    ]
    return jnp.concatenate(pieces, axis=1)


def split(value):
    top = value.astype(BF)
    return top, (value - top.astype(F32)).astype(BF)


def tables(uv_ref, u_tab, v_tab, width):
    scale = -1.0 / width
    a_one, b_one = half_turn(uv_ref[:, 0, :] * scale)
    c_one, d_one = half_turn(uv_ref[:, 1, :] * scale)
    phase_r = a_one * c_one - b_one * d_one
    phase_i = -a_one * d_one - b_one * c_one
    half = width // 2
    twice = 4.0 * a_one * a_one - 2.0
    before, now = a_one, a_one
    before_s, now_s = -b_one, b_one
    for j in range(half):
        lay(u_tab, j, width, now)
        lay(u_tab, half + j, width, now_s)
        before, now = now, twice * now - before
        before_s, now_s = now_s, twice * now_s - before_s

    def put(row, value):
        lay(v_tab, row, 16, value)

    c_square = c_one * c_one
    turn = 4.0 * c_square - 2.0
    put(0, c_one)
    put(2, d_one)
    put(1, turn * c_one - c_one)
    put(3, turn * d_one + d_one)
    r_one, i_one = 2.0 * c_square - 1.0, 2.0 * c_one * d_one
    r_two, i_two = 2.0 * r_one * r_one - 1.0, 2.0 * r_one * i_one
    turn = 8.0 * r_two * r_two - 4.0
    turn = 0.5 * turn
    before, now = r_two, r_two
    before_s, now_s = -i_two, i_two
    for n in range(4):
        put(4 + n, now)
        put(8 + n, now_s)
        before, now = now, turn * now - before
        before_s, now_s = now_s, turn * now_s - before_s
    put(12, phase_r)
    put(13, phase_i)


def swap_parts(value):
    return jnp.concatenate([value[4:8], value[0:4]], axis=0)


def block_kernel(pos_ref, plane_ref, obs_ref, uv_ref, wgt_ref, tile_ref, left_ref, leftt_ref, right_ref,
                 res_ref, out_ref, u_tab, v_tab, prod, grown, coef, vis):
    width = 32
    step = pl.program_id(0)
    tables(uv_ref, u_tab, v_tab, width)
    sign = jnp.where(lax.broadcasted_iota(jnp.int32, (8, CHUNK), 0) < 4, -1.0, 1.0).astype(F32)
    for b in range(STEP):
        index = step * STEP + b
        plane = plane_ref[index]
        tile = tile_ref[pos_ref[index]].reshape(64, 128)
        left = nn_dot(left_ref[plane], tile)
        r_up, r_lo, i_up, i_lo = left[0:16], left[16:32], left[32:48], left[48:64]
        left = jnp.concatenate(
            [
                jnp.concatenate([r_up + r_lo, i_lo - i_up], axis=0),
                jnp.concatenate([i_up + i_lo, r_up - r_lo], axis=0),
            ],
            axis=1,
        )
        top, rest = split(left)
        both = jnp.concatenate([top, rest], axis=0)
        for r in range(4):
            found = nn_dot(both, right_ref[plane, r])
            found = found[:32] + found[32:] + nn_dot(top, right_ref[plane, 4 + r])
            coef[b, 32 * r:32 * r + 32, :] = found.astype(BF)
    for b in range(STEP):
        for start in range(0, 1024, CHUNK):
            lanes = slice(start, start + CHUNK)
            table = rows_of(u_tab, width * b, width, start, width)
            for r in range(4):
                row = rows_of(v_tab, 16 * b + r, 1, start, width)
                prod[b, width * r:width * r + width, lanes] = (table * row).astype(BF)
        spread_rows = coef[b]
        for start in range(0, 1024, CHUNK):
            lanes = slice(start, start + CHUNK)
            spread = tn_dot(spread_rows, prod[b, :, lanes])

            def row_of(r):
                return rows_of(v_tab, 16 * b + r, 1, start, 8)

            total = spread[0:8] * row_of(4)
            for g in range(1, 8):
                total = total + spread[8 * g:8 * g + 8] * row_of(4 + g)
            phase_r, phase_i = row_of(12), row_of(13) * sign
            total = (total * phase_r + swap_parts(total) * phase_i) * (1.0 / width)
            seen = jnp.concatenate([obs_ref[b, 0, :, lanes], obs_ref[b, 1, :, lanes]], axis=0)
            resid = seen - total
            res_ref[b, 0, :, lanes] = resid[0:4]
            res_ref[b, 1, :, lanes] = resid[4:8]
            scaled = resid * (jnp.broadcast_to(wgt_ref[b:b + 1, lanes], (8, CHUNK)) * (1.0 / width))
            turned = scaled * phase_r - swap_parts(scaled) * phase_i
            for g in range(0, 8, 2):
                pair = jnp.concatenate([turned * row_of(4 + g), turned * row_of(5 + g)], axis=0)
                vis[b, 8 * g:8 * g + 16, lanes] = pair.astype(BF)
        grown[b] = nt_dot(prod[b], vis[b])
    for b in range(STEP):
        index = step * STEP + b
        plane = plane_ref[index]
        back = None
        for r in range(4):
            top, rest = split(grown[b, 32 * r:32 * r + 32, :])
            both = jnp.concatenate([top, rest], axis=0)
            found = nt_dot(both, right_ref[plane, r])
            found = found[:32] + found[32:] + nt_dot(top, right_ref[plane, 4 + r])
            back = found if back is None else back + found
        a_r, b_r, a_i, b_i = back[:16, :128], back[16:, :128], back[:16, 128:], back[16:, 128:]
        back = jnp.concatenate([a_r + b_i, a_r - b_i, a_i - b_r, a_i + b_r], axis=0)
        top, rest = split(back)
        contrib = nn_dot(leftt_ref[plane], jnp.concatenate([top, rest], axis=1))
        contrib = contrib[:, :128] + contrib[:, 128:]
        out_ref[pos_ref[index]] = contrib.astype(BF).reshape(2, 32, 128)


def plane_matrices(w_kernels):
    planes, _, width, _ = w_kernels.shape
    half = width // 2
    turned = jnp.concatenate([w_kernels[:, :, half:], w_kernels[:, :, half - 1::-1]], axis=2)
    kr, ki = turned[:, 0], turned[:, 1]
    left = jnp.concatenate([jnp.concatenate([kr, -ki], axis=2), jnp.concatenate([ki, kr], axis=2)], axis=1)
    mix = np.zeros((4, 8, width), np.complex64)
    for r in range(4):
        for g in range(8):
            for s1 in (1, -1):
                for s3 in (1, -1):
                    i, n = r % 2, g % 4
                    m1 = 4 + n if s1 > 0 else 3 - n
                    m2 = 2 + i if s3 > 0 else 1 - i
                    mix[r, g, 4 * m1 + m2] = (1j * s3 if r >= 2 else 1) * (1j * s1 if g >= 4 else 1)
    spread = np.zeros((2, width, 4, 2, 8, 2, 4), np.float32)
    for into in range(2):
        for outof in range(2):
            for src in range(2):
                unit = 1j if src else 1
                factor = mix * unit
                if into == 0 and outof == 0:
                    value = factor.real
                elif into == 0 and outof == 1:
                    value = factor.imag
                elif into == 1 and outof == 0:
                    value = -factor.imag
                else:
                    value = factor.real
                spread[src, :, :, into, :, outof, :] = value.transpose(2, 0, 1)[:, :, :, None]
    spread = spread.reshape(2, width, 4 * 2 * 64)
    grid = jnp.einsum("zcmk,cmq->zkq", w_kernels, jnp.asarray(spread, BF), preferred_element_type=F32)
    top = lax.reduce_precision(grid, 8, 7)
    grid = jnp.stack([top.astype(BF), (grid - top).astype(BF)], axis=1).reshape(planes, 2, width, 4, 2, 64).transpose(0, 1, 3, 4, 2, 5)
    grid = grid.reshape(planes, 8, 2, width, 64)
    pol = np.arange(64) % 4
    mask = (pol[None, :] == np.arange(4)[:, None])[None, None, None, :, None, :]
    right = jnp.where(jnp.asarray(mask), grid[:, :, :, None, :, :], jnp.zeros((), BF))
    right = right.reshape(planes, 8, 256, 64)
    return left, left.transpose(0, 2, 1), right


def degrid_grid(position, w_plane, vis_obs, uv_coords, vis_weight, arrived, left, leftt, right):
    blocks = vis_obs.shape[0]
    grid = blocks // STEP
    whole = lambda *shape: pl.BlockSpec(shape, lambda i, *_: (0,) * len(shape), pipeline_mode=pl.Buffered(1))
    return pl.pallas_call(
        block_kernel,
        grid_spec=pltpu.PrefetchScalarGridSpec(
            num_scalar_prefetch=2,
            grid=(grid,),
            in_specs=[
                pl.BlockSpec((STEP, 2, 4, 1024), lambda i, *_: (i, 0, 0, 0)),
                pl.BlockSpec((STEP, 2, 1024), lambda i, *_: (i, 0, 0)),
                pl.BlockSpec((STEP, 1024), lambda i, *_: (i, 0)),
                whole(*arrived.shape),
                whole(*left.shape),
                whole(*leftt.shape),
                whole(*right.shape),
            ],
            out_specs=[
                pl.BlockSpec((STEP, 2, 4, 1024), lambda i, *_: (i, 0, 0, 0)),
                whole(*arrived.shape),
            ],
            scratch_shapes=[
                pltpu.VMEM((8, STEP * 32, 128), F32),
                pltpu.VMEM((8, STEP * 16, 128), F32),
                pltpu.VMEM((STEP, 128, 1024), BF),
                pltpu.VMEM((STEP, 128, 64), F32),
                pltpu.VMEM((STEP, 128, 64), BF),
                pltpu.VMEM((STEP, 64, 1024), BF),
            ],
        ),
        out_shape=[
            jax.ShapeDtypeStruct(vis_obs.shape, F32),
            jax.ShapeDtypeStruct(arrived.shape, BF),
        ],
        compiler_params=pltpu.CompilerParams(vmem_limit_bytes=60 << 20),
        name="degrid_grid",
    )(position, w_plane, vis_obs, uv_coords, vis_weight, arrived, left, leftt, right)


def sum_kernel(slot_ref, scale_ref, part_ref, out_ref, total):
    step = pl.program_id(0)
    count = part_ref.shape[0]

    @pl.when(step == 0)
    def _():
        total[...] = jnp.zeros_like(total)

    def add(i, carry):
        slot = slot_ref[step * count + i]
        total[slot] = total[slot] + part_ref[i].astype(F32)
        return carry

    lax.fori_loop(0, count, add, 0, unroll=4)

    @pl.when(step == pl.num_programs(0) - 1)
    def _():
        out_ref[...] = total[: out_ref.shape[0]] * scale_ref[0]


def sum_slots(slots, scale, parts, owned):
    count = parts.shape[0] // 8
    shape = parts.shape[1:]
    return pl.pallas_call(
        sum_kernel,
        grid_spec=pltpu.PrefetchScalarGridSpec(
            num_scalar_prefetch=2,
            grid=(8,),
            in_specs=[pl.BlockSpec((count,) + shape, lambda i, *_: (i, 0, 0, 0))],
            out_specs=pl.BlockSpec((owned,) + shape, lambda i, *_: (0, 0, 0, 0)),
            scratch_shapes=[pltpu.VMEM((owned + 1,) + shape, F32)],
        ),
        out_shape=jax.ShapeDtypeStruct((owned,) + shape, F32),
        compiler_params=pltpu.CompilerParams(vmem_limit_bytes=32 << 20),
        name="sum_slots",
    )(slots, scale, parts)


def shards(vis_obs, uv_coords, vis_weight, block_group, tile_slot, w_plane, model_tiles, w_kernels):
    blocks, nvis = vis_weight.shape
    groups = lax.axis_size(AXES)
    owned = model_tiles.shape[0]
    tile_shape = model_tiles.shape[1:]
    target = block_group[:, 0]
    same = target[:, None] == target[None, :]
    earlier = np.arange(blocks)[:, None] > np.arange(blocks)[None, :]
    rank = jnp.sum(same & earlier, axis=1, dtype=jnp.int32)
    position = target * CAP + rank
    wanted = jnp.max(
        jnp.where(
            position[:, None] == jnp.arange(groups * CAP, dtype=jnp.int32)[None, :], tile_slot[:, None], -1
        ),
        axis=0,
    )
    message = jnp.concatenate(
        [wanted.astype(F32).reshape(groups, CAP), jnp.full((groups, 1), jnp.sum(vis_weight))], axis=1
    )
    message = lax.all_to_all(message, AXES, split_axis=0, concat_axis=0, tiled=True)
    requested = message[:, :CAP].astype(jnp.int32).reshape(-1)
    scale = (blocks * groups * nvis) / jnp.sum(message[:, CAP])
    chosen = jnp.take(model_tiles, jnp.maximum(requested, 0), axis=0, mode="clip")
    chosen = chosen.reshape((groups, CAP) + tile_shape)
    arrived = lax.all_to_all(chosen, AXES, split_axis=0, concat_axis=0, tiled=True)
    arrived = arrived.reshape((groups * CAP,) + tile_shape)
    left, leftt, right = plane_matrices(w_kernels)
    residual, outgoing = degrid_grid(
        position, w_plane, vis_obs, uv_coords, vis_weight, arrived, left, leftt, right
    )
    outgoing = outgoing.reshape((groups, CAP) + tile_shape)
    returned = lax.all_to_all(outgoing, AXES, split_axis=0, concat_axis=0, tiled=True)
    returned = returned.reshape((groups * CAP,) + tile_shape)
    slots = jnp.where(requested < 0, owned, requested)
    return residual, sum_slots(slots, scale.reshape(1), returned, owned)


def solution(mesh):
    return jax.shard_map(
        shards,
        mesh=mesh,
        in_specs=(
            P(AXES, None, None, None),
            P(AXES, None, None),
            P(AXES, None),
            P(AXES, None),
            P(AXES),
            P(AXES),
            P(AXES, None, None, None),
            P(),
        ),
        out_specs=(P(AXES, None, None, None), P(AXES, None, None, None)),
        check_vma=False,
    )
```

```python
import jax
import jax.numpy as jnp
import numpy as np
from jax import lax
from jax.experimental import pallas as pl
from jax.experimental.pallas import tpu as pltpu
from jax.sharding import PartitionSpec as P

AXES = ("facet", "vis")
CAP = 2

BF = jnp.bfloat16
F32 = jnp.float32
STEP = 8
CHUNK = 256


def even_fit(func, terms):
    nodes = np.cos(np.pi * (np.arange(200) + 0.5) / 200) * 0.25
    squares = (nodes + 0.25) / 2
    powers = squares[:, None] ** np.arange(terms)[None, :]
    scale = powers.max(axis=0)
    solved = np.linalg.lstsq(powers / scale, func(np.sqrt(squares)), rcond=None)[0]
    return [float(value) for value in solved / scale]


COS_TERMS = even_fit(lambda t: np.cos(np.pi * t), 7)
SIN_TERMS = even_fit(lambda t: np.sin(np.pi * t) / t, 6)


def half_turn(t):
    square = t * t
    cosine = jnp.full_like(t, COS_TERMS[-1])
    for term in COS_TERMS[-2::-1]:
        cosine = cosine * square + term
    sine = jnp.full_like(t, SIN_TERMS[-1])
    for term in SIN_TERMS[-2::-1]:
        sine = sine * square + term
    return cosine, sine * t


def nt_dot(left, right):
    return lax.dot_general(left, right, (((1,), (1,)), ((), ())), preferred_element_type=F32)


def tn_dot(left, right):
    return lax.dot_general(left, right, (((0,), (0,)), ((), ())), preferred_element_type=F32)


def nn_dot(left, right):
    return jnp.dot(left, right, preferred_element_type=F32)


def lay(table, row, value):
    for t in range(value.shape[1] // 128):
        table[t, STEP * row:STEP * row + STEP, :] = value[:, 128 * t:128 * t + 128]


def column(table, b, start):
    pieces = [table[start // 128 + t, pl.ds(b, 32, stride=STEP), :] for t in range(CHUNK // 128)]
    return jnp.concatenate(pieces, axis=1)


def row_of(table, row, b, start, count):
    first = STEP * row + b
    pieces = [
        jnp.broadcast_to(table[start // 128 + t, first:first + 1, :], (count, 128))
        for t in range(CHUNK // 128)
    ]
    return jnp.concatenate(pieces, axis=1)


def split(value):
    top = value.astype(BF)
    return top, (value - top.astype(F32)).astype(BF)


def tables(uv_ref, u_tab, v_tab, width):
    scale = -1.0 / width
    a_one, b_one = half_turn(uv_ref[0] * scale)
    c_one, d_one = half_turn(uv_ref[1] * scale)
    phase_r = (a_one * c_one - b_one * d_one)
    phase_i = -a_one * d_one - b_one * c_one
    half = width // 2
    twice = 4.0 * a_one * a_one - 2.0
    before, now = a_one, a_one
    before_s, now_s = -b_one, b_one
    for j in range(half):
        lay(u_tab, j, now)
        lay(u_tab, half + j, now_s)
        before, now = now, twice * now - before
        before_s, now_s = now_s, twice * now_s - before_s

    def put(row, value):
        lay(v_tab, row, value)

    c_square = c_one * c_one
    turn = 4.0 * c_square - 2.0
    put(0, c_one)
    put(2, d_one)
    put(1, turn * c_one - c_one)
    put(3, turn * d_one + d_one)
    r_one, i_one = 2.0 * c_square - 1.0, 2.0 * c_one * d_one
    r_two, i_two = 2.0 * r_one * r_one - 1.0, 2.0 * r_one * i_one
    turn = 4.0 * r_two * r_two - 2.0
    before, now = r_two, r_two
    before_s, now_s = -i_two, i_two
    for n in range(4):
        put(4 + n, now)
        put(8 + n, now_s)
        before, now = now, turn * now - before
        before_s, now_s = now_s, turn * now_s - before_s
    put(12, phase_r)
    put(13, phase_i)


def swap_parts(value):
    return pltpu.roll(value, 4, 0)


def forward(b, tile, left_k, right_top, right_rest, coef):
    left = nn_dot(left_k, tile.reshape(64, 128))
    r_up, r_lo, i_up, i_lo = left[0:16], left[16:32], left[32:48], left[48:64]
    left = jnp.concatenate(
        [
            jnp.concatenate([r_up + r_lo, i_lo - i_up], axis=0),
            jnp.concatenate([i_up + i_lo, r_up - r_lo], axis=0),
        ],
        axis=1,
    )
    top, rest = split(left)
    found = nn_dot(jnp.concatenate([top, rest], axis=0), right_top)
    found = found[:32] + found[32:] + nn_dot(top, right_rest)
    for r in range(4):
        coef[b, 32 * r:32 * r + 32, :] = found[:, 64 * r:64 * r + 64].astype(BF)


def backward(grown, left_k, right_top, right_rest):
    grown = jnp.concatenate([grown[32 * r:32 * r + 32] for r in range(4)], axis=1)
    top, rest = split(grown)
    back = nt_dot(jnp.concatenate([top, rest], axis=0), right_top)
    back = back[:32] + back[32:] + nt_dot(top, right_rest)
    a_r, b_r, a_i, b_i = back[:16, :128], back[16:, :128], back[:16, 128:], back[16:, 128:]
    back = jnp.concatenate([a_r + b_i, a_r - b_i, a_i - b_r, a_i + b_r], axis=0)
    top, rest = split(back)
    contrib = nn_dot(left_k, jnp.concatenate([top, rest], axis=1))
    return (contrib[:, :128] + contrib[:, 128:]).astype(BF).reshape(2, 32, 128)


def block_kernel(pos_ref, plane_ref, obs_ref, uv_ref, wgt_ref, tile_ref, left_ref, leftt_ref, right_ref,
                 res_ref, out_ref, u_tab, v_tab, prod, grown, coef, vis):
    width = 32
    step = pl.program_id(0)
    tables(uv_ref, u_tab, v_tab, width)
    sign = jnp.where(lax.broadcasted_iota(jnp.int32, (8, CHUNK), 0) < 4, -1.0, 1.0).astype(F32)

    def first(b):
        index = step * STEP + b
        plane = plane_ref[index]
        forward(b, tile_ref[pos_ref[index]], left_ref[plane], right_ref[plane, 0], right_ref[plane, 1], coef)

    def products(b):
        for start in range(0, 1024, CHUNK):
            lanes = slice(start, start + CHUNK)
            table = column(u_tab, b, start)
            for r in range(4):
                row = row_of(v_tab, r, b, start, width)
                prod[b, width * r:width * r + width, lanes] = (table * row).astype(BF)

    def middle(b):
        for start in range(0, 1024, CHUNK):
            lanes = slice(start, start + CHUNK)
            spread = tn_dot(coef[b], prod[b, :, lanes])
            rows = [row_of(v_tab, 4 + g, b, start, 8) for g in range(8)]
            total = spread[0:8] * rows[0]
            for g in range(1, 8):
                total = total + spread[8 * g:8 * g + 8] * rows[g]
            phase_r, phase_i = row_of(v_tab, 12, b, start, 8), row_of(v_tab, 13, b, start, 8) * sign
            total = total * phase_r + swap_parts(total) * phase_i
            resid = obs_ref[b, :, lanes] - total
            res_ref[b, :, lanes] = resid
            scaled = resid * jnp.broadcast_to(wgt_ref[b:b + 1, lanes], (8, CHUNK))
            turned = scaled * phase_r - swap_parts(scaled) * phase_i
            for g in range(0, 8, 2):
                pair = jnp.concatenate([turned * rows[g], turned * rows[g + 1]], axis=0)
                vis[b, 8 * g:8 * g + 16, lanes] = pair.astype(BF)
        grown[b] = nt_dot(prod[b], vis[b])

    def last(b):
        index = step * STEP + b
        plane = plane_ref[index]
        out_ref[pos_ref[index]] = backward(grown[b], leftt_ref[plane], right_ref[plane, 0], right_ref[plane, 1])

    for turn in range(STEP + 2):
        if turn < STEP:
            first(turn)
            products(turn)
        if 0 <= turn - 1 < STEP:
            middle(turn - 1)
        if 0 <= turn - 2 < STEP:
            last(turn - 2)


def plane_matrices(w_kernels):
    planes, _, width, _ = w_kernels.shape
    half = width // 2
    turned = jnp.concatenate([w_kernels[:, :, half:], w_kernels[:, :, half - 1::-1]], axis=2)
    kr, ki = turned[:, 0], turned[:, 1]
    left = jnp.concatenate([jnp.concatenate([kr, -ki], axis=2), jnp.concatenate([ki, kr], axis=2)], axis=1)
    mix = np.zeros((4, 8, width), np.complex64)
    for r in range(4):
        for g in range(8):
            for s1 in (1, -1):
                for s3 in (1, -1):
                    i, n = r % 2, g % 4
                    m1 = 4 + n if s1 > 0 else 3 - n
                    m2 = 2 + i if s3 > 0 else 1 - i
                    mix[r, g, 4 * m1 + m2] = (1j * s3 if r >= 2 else 1) * (1j * s1 if g >= 4 else 1)
    spread = np.zeros((2, width, 2, 4, 8, 2, 4), np.float32)
    for into in range(2):
        for outof in range(2):
            for src in range(2):
                unit = 1j if src else 1
                factor = mix * unit
                if into == 0 and outof == 0:
                    value = factor.real
                elif into == 0 and outof == 1:
                    value = factor.imag
                elif into == 1 and outof == 0:
                    value = -factor.imag
                else:
                    value = factor.real
                spread[src, :, into, :, :, outof, :] = value.transpose(2, 0, 1)[:, :, :, None]
    spread = spread.reshape(2, width, 512)
    grid = jnp.einsum("zcmk,cmq->zkq", w_kernels, jnp.asarray(spread, BF), preferred_element_type=F32)
    grid = grid * (1.0 / width)
    top = lax.reduce_precision(grid, 8, 7)
    grid = jnp.stack([top.astype(BF), (grid - top).astype(BF)], axis=1)
    grid = grid.reshape(planes, 2, width, 2, 256).transpose(0, 1, 3, 2, 4)
    pol = np.arange(256) % 4
    mask = (pol[None, :] == np.arange(4)[:, None])[None, None, None, :, None, :]
    right = jnp.where(jnp.asarray(mask), grid[:, :, :, None, :, :], jnp.zeros((), BF))
    right = right.reshape(planes, 2, 256, 256)
    return left, left.transpose(0, 2, 1), right


def degrid_grid(position, w_plane, vis_obs, uv_coords, vis_weight, arrived, left, leftt, right):
    blocks = vis_obs.shape[0]
    grid = blocks // STEP
    vis_obs = vis_obs.reshape(blocks, 8, 1024)
    uv_coords = uv_coords.transpose(1, 0, 2)
    whole = lambda *shape: pl.BlockSpec(shape, lambda i, *_: (0,) * len(shape), pipeline_mode=pl.Buffered(1))
    residual, outgoing = pl.pallas_call(
        block_kernel,
        grid_spec=pltpu.PrefetchScalarGridSpec(
            num_scalar_prefetch=2,
            grid=(grid,),
            in_specs=[
                pl.BlockSpec((STEP, 8, 1024), lambda i, *_: (i, 0, 0)),
                pl.BlockSpec((2, STEP, 1024), lambda i, *_: (0, i, 0)),
                pl.BlockSpec((STEP, 1024), lambda i, *_: (i, 0)),
                whole(*arrived.shape),
                whole(*left.shape),
                whole(*leftt.shape),
                whole(*right.shape),
            ],
            out_specs=[
                pl.BlockSpec((STEP, 8, 1024), lambda i, *_: (i, 0, 0)),
                whole(*arrived.shape),
            ],
            scratch_shapes=[
                pltpu.VMEM((8, 32 * STEP, 128), F32),
                pltpu.VMEM((8, 16 * STEP, 128), F32),
                pltpu.VMEM((STEP, 128, 1024), BF),
                pltpu.VMEM((STEP, 128, 64), F32),
                pltpu.VMEM((STEP, 128, 64), BF),
                pltpu.VMEM((STEP, 64, 1024), BF),
            ],
        ),
        out_shape=[
            jax.ShapeDtypeStruct(vis_obs.shape, F32),
            jax.ShapeDtypeStruct(arrived.shape, BF),
        ],
        compiler_params=pltpu.CompilerParams(vmem_limit_bytes=60 << 20),
        name="degrid_grid",
    )(position, w_plane, vis_obs, uv_coords, vis_weight, arrived, left, leftt, right)
    return residual.reshape(blocks, 2, 4, 1024), outgoing


def sum_kernel(slot_ref, scale_ref, part_ref, out_ref, total):
    step = pl.program_id(0)
    count = part_ref.shape[0]

    @pl.when(step == 0)
    def _():
        total[...] = jnp.zeros_like(total)

    def add(i, carry):
        slot = slot_ref[step * count + i]
        total[slot] = total[slot] + part_ref[i].astype(F32)
        return carry

    lax.fori_loop(0, count, add, 0, unroll=4)

    @pl.when(step == pl.num_programs(0) - 1)
    def _():
        out_ref[...] = total[: out_ref.shape[0]] * scale_ref[0]


def sum_slots(slots, scale, parts, owned):
    count = parts.shape[0] // 8
    shape = parts.shape[1:]
    return pl.pallas_call(
        sum_kernel,
        grid_spec=pltpu.PrefetchScalarGridSpec(
            num_scalar_prefetch=2,
            grid=(8,),
            in_specs=[pl.BlockSpec((count,) + shape, lambda i, *_: (i, 0, 0, 0))],
            out_specs=pl.BlockSpec((owned,) + shape, lambda i, *_: (0, 0, 0, 0)),
            scratch_shapes=[pltpu.VMEM((owned + 1,) + shape, F32)],
        ),
        out_shape=jax.ShapeDtypeStruct((owned,) + shape, F32),
        compiler_params=pltpu.CompilerParams(vmem_limit_bytes=32 << 20),
        name="sum_slots",
    )(slots, scale, parts)


def shards(vis_obs, uv_coords, vis_weight, block_group, tile_slot, w_plane, model_tiles, w_kernels):
    blocks, nvis = vis_weight.shape
    groups = lax.axis_size(AXES)
    owned = model_tiles.shape[0]
    tile_shape = model_tiles.shape[1:]
    target = block_group[:, 0]
    same = target[:, None] == target[None, :]
    earlier = np.arange(blocks)[:, None] > np.arange(blocks)[None, :]
    rank = jnp.sum(same & earlier, axis=1, dtype=jnp.int32)
    position = target * CAP + rank
    wanted = jnp.max(
        jnp.where(
            position[:, None] == jnp.arange(groups * CAP, dtype=jnp.int32)[None, :], tile_slot[:, None], -1
        ),
        axis=0,
    )
    message = jnp.concatenate(
        [wanted.astype(F32).reshape(groups, CAP), jnp.full((groups, 1), jnp.sum(vis_weight))], axis=1
    )
    message = lax.all_to_all(message, AXES, split_axis=0, concat_axis=0, tiled=True)
    requested = message[:, :CAP].astype(jnp.int32).reshape(-1)
    scale = (blocks * groups * nvis) / jnp.sum(message[:, CAP])
    chosen = jnp.take(model_tiles, jnp.maximum(requested, 0), axis=0, mode="clip")
    chosen = chosen.reshape((groups, CAP) + tile_shape)
    arrived = lax.all_to_all(chosen, AXES, split_axis=0, concat_axis=0, tiled=True)
    arrived = arrived.reshape((groups * CAP,) + tile_shape)
    left, leftt, right = plane_matrices(w_kernels)
    residual, outgoing = degrid_grid(
        position, w_plane, vis_obs, uv_coords, vis_weight, arrived, left, leftt, right
    )
    outgoing = outgoing.reshape((groups, CAP) + tile_shape)
    returned = lax.all_to_all(outgoing, AXES, split_axis=0, concat_axis=0, tiled=True)
    returned = returned.reshape((groups * CAP,) + tile_shape)
    slots = jnp.where(requested < 0, owned, requested)
    return residual, sum_slots(slots, scale.reshape(1), returned, owned)


def solution(mesh):
    return jax.shard_map(
        shards,
        mesh=mesh,
        in_specs=(
            P(AXES, None, None, None),
            P(AXES, None, None),
            P(AXES, None),
            P(AXES, None),
            P(AXES),
            P(AXES),
            P(AXES, None, None, None),
            P(),
        ),
        out_specs=(P(AXES, None, None, None), P(AXES, None, None, None)),
        check_vma=False,
    )
```

```python
import jax
import jax.numpy as jnp
import numpy as np
from jax import lax
from jax.experimental import pallas as pl
from jax.experimental.pallas import tpu as pltpu
from jax.sharding import PartitionSpec as P

AXES = ("facet", "vis")

BF = jnp.bfloat16
F32 = jnp.float32
STEP = 8
CHUNK = 256


def even_fit(func, terms):
    nodes = np.cos(np.pi * (np.arange(200) + 0.5) / 200) * 0.25
    squares = (nodes + 0.25) / 2
    powers = squares[:, None] ** np.arange(terms)[None, :]
    scale = powers.max(axis=0)
    solved = np.linalg.lstsq(powers / scale, func(np.sqrt(squares)), rcond=None)[0]
    return [float(value) for value in solved / scale]


COS_TERMS = even_fit(lambda t: np.cos(np.pi * t), 7)
SIN_TERMS = even_fit(lambda t: np.sin(np.pi * t) / t, 6)


def half_turn(t):
    square = t * t
    cosine = jnp.full_like(t, COS_TERMS[-1])
    for term in COS_TERMS[-2::-1]:
        cosine = cosine * square + term
    sine = jnp.full_like(t, SIN_TERMS[-1])
    for term in SIN_TERMS[-2::-1]:
        sine = sine * square + term
    return cosine, sine * t


def nt_dot(left, right):
    return lax.dot_general(left, right, (((1,), (1,)), ((), ())), preferred_element_type=F32)


def tn_dot(left, right):
    return lax.dot_general(left, right, (((0,), (0,)), ((), ())), preferred_element_type=F32)


def nn_dot(left, right):
    return jnp.dot(left, right, preferred_element_type=F32)


def lay(table, row, value):
    for t in range(value.shape[1] // 128):
        table[t, STEP * row:STEP * row + STEP, :] = value[:, 128 * t:128 * t + 128]


def column(table, b, start):
    pieces = [table[start // 128 + t, pl.ds(b, 32, stride=STEP), :] for t in range(CHUNK // 128)]
    return jnp.concatenate(pieces, axis=1)


def row_of(table, row, b, start, count):
    first = STEP * row + b
    pieces = [
        jnp.broadcast_to(table[start // 128 + t, first:first + 1, :], (count, 128))
        for t in range(CHUNK // 128)
    ]
    return jnp.concatenate(pieces, axis=1)


def split(value):
    top = value.astype(BF)
    return top, (value - top.astype(F32)).astype(BF)


def tables(uv_ref, u_tab, v_tab, width):
    scale = -1.0 / width
    a_one, b_one = half_turn(uv_ref[0] * scale)
    c_one, d_one = half_turn(uv_ref[1] * scale)
    phase_r = (a_one * c_one - b_one * d_one)
    phase_i = -a_one * d_one - b_one * c_one
    half = width // 2
    twice = 4.0 * a_one * a_one - 2.0
    before, now = a_one, a_one
    before_s, now_s = -b_one, b_one
    for j in range(half):
        lay(u_tab, j, now)
        lay(u_tab, half + j, now_s)
        before, now = now, twice * now - before
        before_s, now_s = now_s, twice * now_s - before_s

    def put(row, value):
        lay(v_tab, row, value)

    c_square = c_one * c_one
    turn = 4.0 * c_square - 2.0
    put(0, c_one)
    put(2, d_one)
    put(1, turn * c_one - c_one)
    put(3, turn * d_one + d_one)
    r_one, i_one = 2.0 * c_square - 1.0, 2.0 * c_one * d_one
    r_two, i_two = 2.0 * r_one * r_one - 1.0, 2.0 * r_one * i_one
    turn = 4.0 * r_two * r_two - 2.0
    before, now = r_two, r_two
    before_s, now_s = -i_two, i_two
    for n in range(4):
        put(4 + n, now)
        put(8 + n, now_s)
        before, now = now, turn * now - before
        before_s, now_s = now_s, turn * now_s - before_s
    put(12, phase_r)
    put(13, phase_i)


def swap_parts(value):
    return pltpu.roll(value, 4, 0)


def forward(b, tile, left_k, right_top, right_rest, coef):
    left = nn_dot(left_k, tile.reshape(64, 128))
    r_up, r_lo, i_up, i_lo = left[0:16], left[16:32], left[32:48], left[48:64]
    left = jnp.concatenate(
        [
            jnp.concatenate([r_up + r_lo, i_lo - i_up], axis=0),
            jnp.concatenate([i_up + i_lo, r_up - r_lo], axis=0),
        ],
        axis=1,
    )
    top, rest = split(left)
    found = nn_dot(jnp.concatenate([top, rest], axis=0), right_top)
    found = found[:32] + found[32:] + nn_dot(top, right_rest)
    for r in range(4):
        coef[b, 32 * r:32 * r + 32, :] = found[:, 64 * r:64 * r + 64].astype(BF)


def backward(grown, left_k, right_top, right_rest):
    grown = jnp.concatenate([grown[32 * r:32 * r + 32] for r in range(4)], axis=1)
    top, rest = split(grown)
    back = nt_dot(jnp.concatenate([top, rest], axis=0), right_top)
    back = back[:32] + back[32:] + nt_dot(top, right_rest)
    a_r, b_r, a_i, b_i = back[:16, :128], back[16:, :128], back[:16, 128:], back[16:, 128:]
    back = jnp.concatenate([a_r + b_i, a_r - b_i, a_i - b_r, a_i + b_r], axis=0)
    top, rest = split(back)
    contrib = nn_dot(left_k, jnp.concatenate([top, rest], axis=1))
    return (contrib[:, :128] + contrib[:, 128:]).astype(BF).reshape(2, 32, 128)


def block_kernel(order_ref, pos_ref, plane_ref, *refs):
    obs_refs = refs[:STEP]
    uv_ref, wgt_ref, tile_ref, left_ref, leftt_ref, right_ref = refs[STEP:STEP + 6]
    res_ref, out_ref, u_tab, v_tab, prod, grown, coef, vis = refs[-8:]
    width = 32
    step = pl.program_id(0)
    tables(uv_ref, u_tab, v_tab, width)
    sign = jnp.where(lax.broadcasted_iota(jnp.int32, (8, CHUNK), 0) < 4, -1.0, 1.0).astype(F32)

    def first(b):
        index = step * STEP + b
        plane = plane_ref[index]
        forward(b, tile_ref[pos_ref[index]], left_ref[plane], right_ref[plane, 0], right_ref[plane, 1], coef)

    def products(b):
        for start in range(0, 1024, CHUNK):
            lanes = slice(start, start + CHUNK)
            table = column(u_tab, b, start)
            for r in range(4):
                row = row_of(v_tab, r, b, start, width)
                prod[b, width * r:width * r + width, lanes] = (table * row).astype(BF)

    def middle(b):
        for start in range(0, 1024, CHUNK):
            lanes = slice(start, start + CHUNK)
            spread = tn_dot(coef[b], prod[b, :, lanes])
            rows = [row_of(v_tab, 4 + g, b, start, 8) for g in range(8)]
            total = spread[0:8] * rows[0]
            for g in range(1, 8):
                total = total + spread[8 * g:8 * g + 8] * rows[g]
            phase_r, phase_i = row_of(v_tab, 12, b, start, 8), row_of(v_tab, 13, b, start, 8) * sign
            total = total * phase_r + swap_parts(total) * phase_i
            seen = jnp.concatenate([obs_refs[b][0, 0, :, lanes], obs_refs[b][0, 1, :, lanes]], axis=0)
            resid = seen - total
            res_ref[b, :, lanes] = resid
            scaled = resid * jnp.broadcast_to(wgt_ref[b:b + 1, lanes], (8, CHUNK))
            turned = scaled * phase_r - swap_parts(scaled) * phase_i
            for g in range(0, 8, 2):
                pair = jnp.concatenate([turned * rows[g], turned * rows[g + 1]], axis=0)
                vis[b, 8 * g:8 * g + 16, lanes] = pair.astype(BF)
        grown[b] = nt_dot(prod[b], vis[b])

    def last(b):
        index = step * STEP + b
        plane = plane_ref[index]
        out_ref[pos_ref[index]] = backward(grown[b], leftt_ref[plane], right_ref[plane, 0], right_ref[plane, 1])

    for turn in range(STEP + 2):
        if turn < STEP:
            first(turn)
            products(turn)
        if 0 <= turn - 1 < STEP:
            middle(turn - 1)
        if 0 <= turn - 2 < STEP:
            last(turn - 2)


def plane_matrices(w_kernels):
    planes, _, width, _ = w_kernels.shape
    half = width // 2
    turned = jnp.concatenate([w_kernels[:, :, half:], w_kernels[:, :, half - 1::-1]], axis=2)
    kr, ki = turned[:, 0], turned[:, 1]
    left = jnp.concatenate([jnp.concatenate([kr, -ki], axis=2), jnp.concatenate([ki, kr], axis=2)], axis=1)
    mix = np.zeros((4, 8, width), np.complex64)
    for r in range(4):
        for g in range(8):
            for s1 in (1, -1):
                for s3 in (1, -1):
                    i, n = r % 2, g % 4
                    m1 = 4 + n if s1 > 0 else 3 - n
                    m2 = 2 + i if s3 > 0 else 1 - i
                    mix[r, g, 4 * m1 + m2] = (1j * s3 if r >= 2 else 1) * (1j * s1 if g >= 4 else 1)
    spread = np.zeros((2, width, 2, 4, 8, 2, 4), np.float32)
    for into in range(2):
        for outof in range(2):
            for src in range(2):
                unit = 1j if src else 1
                factor = mix * unit
                if into == 0 and outof == 0:
                    value = factor.real
                elif into == 0 and outof == 1:
                    value = factor.imag
                elif into == 1 and outof == 0:
                    value = -factor.imag
                else:
                    value = factor.real
                spread[src, :, into, :, :, outof, :] = value.transpose(2, 0, 1)[:, :, :, None]
    spread = spread.reshape(2, width, 512)
    grid = jnp.einsum("zcmk,cmq->zkq", w_kernels, jnp.asarray(spread, BF), preferred_element_type=F32)
    grid = grid * (1.0 / width)
    top = lax.reduce_precision(grid, 8, 7)
    grid = jnp.stack([top.astype(BF), (grid - top).astype(BF)], axis=1)
    grid = grid.reshape(planes, 2, width, 2, 256).transpose(0, 1, 3, 2, 4)
    pol = np.arange(256) % 4
    mask = (pol[None, :] == np.arange(4)[:, None])[None, None, None, :, None, :]
    right = jnp.where(jnp.asarray(mask), grid[:, :, :, None, :, :], jnp.zeros((), BF))
    right = right.reshape(planes, 2, 256, 256)
    return left, left.transpose(0, 2, 1), right


def degrid_grid(phase, order, position, planes, vis_obs, uv_coords, vis_weight, arrived, matrices, residual):
    blocks = vis_obs.shape[0]
    count = order.shape[0]
    left, leftt, right = matrices

    def whole(array):
        zeros = (0,) * array.ndim
        return pl.BlockSpec(array.shape, lambda i, *_: zeros, pipeline_mode=pl.Buffered(1))

    def obs_spec(b):
        return pl.BlockSpec((1, 2, 4, 1024), lambda i, order_ref, *_: (order_ref[i * STEP + b], 0, 0, 0))

    steps = count // STEP
    first = phase * steps
    operands = [vis_obs] * STEP + [uv_coords, vis_weight, arrived, left, leftt, right]
    in_specs = [obs_spec(b) for b in range(STEP)] + [
        pl.BlockSpec((2, STEP, 1024), lambda i, *_: (0, i + first, 0)),
        pl.BlockSpec((STEP, 1024), lambda i, *_: (i + first, 0)),
        whole(arrived),
        whole(left),
        whole(leftt),
        whole(right),
    ]
    aliases = {}
    if residual is not None:
        operands.append(residual)
        in_specs.append(pl.BlockSpec(memory_space=pl.ANY))
        aliases = {3 + len(operands) - 1: 0}
    return pl.pallas_call(
        block_kernel,
        grid_spec=pltpu.PrefetchScalarGridSpec(
            num_scalar_prefetch=3,
            grid=(steps,),
            in_specs=in_specs,
            out_specs=[
                pl.BlockSpec((STEP, 8, 1024), lambda i, *_: (i + first, 0, 0)),
                whole(arrived),
            ],
            scratch_shapes=[
                pltpu.VMEM((8, 32 * STEP, 128), F32),
                pltpu.VMEM((8, 16 * STEP, 128), F32),
                pltpu.VMEM((STEP, 128, 1024), BF),
                pltpu.VMEM((STEP, 128, 64), F32),
                pltpu.VMEM((STEP, 128, 64), BF),
                pltpu.VMEM((STEP, 64, 1024), BF),
            ],
        ),
        out_shape=[
            jax.ShapeDtypeStruct((blocks, 8, 1024), F32),
            jax.ShapeDtypeStruct(arrived.shape, BF),
        ],
        input_output_aliases=aliases,
        compiler_params=pltpu.CompilerParams(vmem_limit_bytes=63 << 20),
        cost_estimate=pl.CostEstimate(flops=count * 80_000_000, bytes_accessed=count * 120_000, transcendentals=0),
        name=f"degrid_grid_{phase}",
    )(order, position, planes, *operands)


def sum_kernel(slot_ref, scale_ref, part_ref, start_ref, out_ref, total):
    step = pl.program_id(0)
    count = part_ref.shape[0]

    @pl.when(step == 0)
    def _():
        total[...] = start_ref[...]

    def add(i, carry):
        slot = slot_ref[step * count + i]
        total[slot] = total[slot] + part_ref[i].astype(F32)
        return carry

    lax.fori_loop(0, count, add, 0, unroll=4)

    @pl.when(step == pl.num_programs(0) - 1)
    def _():
        out_ref[...] = total[: out_ref.shape[0]] * scale_ref[0]


def sum_slots(slots, scale, parts, start, rows):
    count = parts.shape[0] // 8
    shape = parts.shape[1:]
    return pl.pallas_call(
        sum_kernel,
        grid_spec=pltpu.PrefetchScalarGridSpec(
            num_scalar_prefetch=2,
            grid=(8,),
            in_specs=[
                pl.BlockSpec((count,) + shape, lambda i, *_: (i, 0, 0, 0)),
                pl.BlockSpec(start.shape, lambda i, *_: (0, 0, 0, 0), pipeline_mode=pl.Buffered(1)),
            ],
            out_specs=pl.BlockSpec((rows,) + shape, lambda i, *_: (0, 0, 0, 0), pipeline_mode=pl.Buffered(1)),
            scratch_shapes=[pltpu.VMEM(start.shape, F32)],
        ),
        out_shape=jax.ShapeDtypeStruct((rows,) + shape, F32),
        compiler_params=pltpu.CompilerParams(vmem_limit_bytes=63 << 20),
        cost_estimate=pl.CostEstimate(flops=4_000_000, bytes_accessed=6_000_000, transcendentals=0),
        name="sum_slots",
    )(slots, scale, parts, start)


def plan(target, blocks):
    same = target[:, None] == target[None, :]
    earlier = np.arange(blocks)[:, None] > np.arange(blocks)[None, :]
    rank = jnp.sum(same & earlier, axis=1, dtype=jnp.int32)
    double = jnp.sum(same, axis=1, dtype=jnp.int32) > 1
    singles = jnp.sum(earlier & ~double[None, :], axis=1, dtype=jnp.int32)
    spare = blocks // 2 - jnp.sum(double, dtype=jnp.int32) // 2
    phase = jnp.where(double, rank, (singles >= spare).astype(jnp.int32))
    return phase, earlier


def shards(vis_obs, uv_coords, vis_weight, block_group, tile_slot, w_plane, model_tiles, w_kernels):
    blocks, nvis = vis_weight.shape
    groups = lax.axis_size(AXES)
    owned = model_tiles.shape[0]
    half = blocks // 2
    target = block_group[:, 0]
    phase, earlier = plan(target, blocks)
    slot = jnp.arange(2 * groups, dtype=jnp.int32)
    wanted = jnp.max(
        jnp.where((target + phase * groups)[None, :] == slot[:, None], tile_slot[None, :], -1), axis=1
    ).reshape(2, groups)
    message = jnp.concatenate(
        [wanted.astype(F32).T, jnp.full((groups, 1), jnp.sum(vis_weight))], axis=1
    )
    message = lax.all_to_all(message, AXES, split_axis=0, concat_axis=0, tiled=True)
    requested = message[:, :2].astype(jnp.int32)
    scale = (blocks * groups * nvis) / jnp.sum(message[:, 2])

    def exchange(array):
        return lax.all_to_all(array, AXES, split_axis=0, concat_axis=0, tiled=True)

    chosen = [
        jnp.take(model_tiles, jnp.maximum(requested[:, turn], 0), axis=0, mode="clip")
        for turn in range(2)
    ]
    arrived = [exchange(chosen[0])]
    place = phase * half + jnp.sum(
        earlier & (phase[:, None] == phase[None, :]), axis=1, dtype=jnp.int32
    )
    at = place[None, :] == jnp.arange(blocks, dtype=jnp.int32)[:, None]

    def ordered(values):
        return jnp.sum(jnp.where(at, values[None, :], 0), axis=1, dtype=jnp.int32)

    order = ordered(jnp.arange(blocks, dtype=jnp.int32))
    position = ordered(target)
    planes = ordered(w_plane)
    uv_sorted = jnp.take(uv_coords.transpose(1, 0, 2), order, axis=1, mode="clip")
    weight_sorted = jnp.take(vis_weight, order, axis=0, mode="clip")
    matrices = plane_matrices(w_kernels)
    late, matrices, uv_sorted, weight_sorted, order, position, planes = lax.optimization_barrier(
        (chosen[1], matrices, uv_sorted, weight_sorted, order, position, planes)
    )
    arrived.append(exchange(late))
    residual = None
    returned = []
    for turn in range(2):
        part = slice(turn * half, turn * half + half)
        residual, outgoing = degrid_grid(
            turn, order[part], position[part], planes[part], vis_obs, uv_sorted, weight_sorted,
            arrived[turn], matrices, residual
        )
        returned.append(exchange(outgoing))
    residual = jnp.take(residual, place, axis=0, mode="clip").reshape(vis_obs.shape)
    slots = jnp.where(requested < 0, owned, requested)
    start = jnp.zeros((owned + 1,) + model_tiles.shape[1:], F32)
    one = jnp.ones((1,), F32)
    partial = sum_slots(slots[:, 0], one, returned[0], start, owned + 1)
    return residual, sum_slots(slots[:, 1], scale.reshape(1), returned[1], partial, owned)


def solution(mesh):
    return jax.shard_map(
        shards,
        mesh=mesh,
        in_specs=(
            P(AXES, None, None, None),
            P(AXES, None, None),
            P(AXES, None),
            P(AXES, None),
            P(AXES),
            P(AXES),
            P(AXES, None, None, None),
            P(),
        ),
        out_specs=(P(AXES, None, None, None), P(AXES, None, None, None)),
        check_vma=False,
    )
```

```python
import jax
import jax.numpy as jnp
import numpy as np
from jax import lax
from jax.experimental import pallas as pl
from jax.experimental.pallas import tpu as pltpu
from jax.sharding import PartitionSpec as P

AXES = ("facet", "vis")

BF = jnp.bfloat16
F32 = jnp.float32
STEP = 8
CHUNK = 256


def even_fit(func, terms):
    nodes = np.cos(np.pi * (np.arange(200) + 0.5) / 200) * 0.25
    squares = (nodes + 0.25) / 2
    powers = squares[:, None] ** np.arange(terms)[None, :]
    scale = powers.max(axis=0)
    solved = np.linalg.lstsq(powers / scale, func(np.sqrt(squares)), rcond=None)[0]
    return [float(value) for value in solved / scale]


COS_TERMS = even_fit(lambda t: np.cos(np.pi * t), 7)
SIN_TERMS = even_fit(lambda t: np.sin(np.pi * t) / t, 6)


def half_turn(t):
    square = t * t
    cosine = jnp.full_like(t, COS_TERMS[-1])
    for term in COS_TERMS[-2::-1]:
        cosine = cosine * square + term
    sine = jnp.full_like(t, SIN_TERMS[-1])
    for term in SIN_TERMS[-2::-1]:
        sine = sine * square + term
    return cosine, sine * t


def nt_dot(left, right):
    return lax.dot_general(left, right, (((1,), (1,)), ((), ())), preferred_element_type=F32)


def tn_dot(left, right):
    return lax.dot_general(left, right, (((0,), (0,)), ((), ())), preferred_element_type=F32)


def nn_dot(left, right):
    return jnp.dot(left, right, preferred_element_type=F32)


def lay(table, row, value):
    for t in range(value.shape[1] // 128):
        table[t, STEP * row:STEP * row + STEP, :] = value[:, 128 * t:128 * t + 128]


def column(table, b, start):
    pieces = [table[start // 128 + t, pl.ds(b, 32, stride=STEP), :] for t in range(CHUNK // 128)]
    return jnp.concatenate(pieces, axis=1)


def row_of(table, row, b, start, count):
    first = STEP * row + b
    pieces = [
        jnp.broadcast_to(table[start // 128 + t, first:first + 1, :], (count, 128))
        for t in range(CHUNK // 128)
    ]
    return jnp.concatenate(pieces, axis=1)


def split(value):
    top = value.astype(BF)
    return top, (value - top.astype(F32)).astype(BF)


def tables(uv_ref, u_tab, v_tab, width):
    scale = -1.0 / width
    a_one, b_one = half_turn(uv_ref[0] * scale)
    c_one, d_one = half_turn(uv_ref[1] * scale)
    phase_r = (a_one * c_one - b_one * d_one)
    phase_i = -a_one * d_one - b_one * c_one
    half = width // 2
    twice = 4.0 * a_one * a_one - 2.0
    before, now = a_one, a_one
    before_s, now_s = -b_one, b_one
    for j in range(half):
        lay(u_tab, j, now)
        lay(u_tab, half + j, now_s)
        before, now = now, twice * now - before
        before_s, now_s = now_s, twice * now_s - before_s

    def put(row, value):
        lay(v_tab, row, value)

    c_square = c_one * c_one
    turn = 4.0 * c_square - 2.0
    put(0, c_one)
    put(2, d_one)
    put(1, turn * c_one - c_one)
    put(3, turn * d_one + d_one)
    r_one, i_one = 2.0 * c_square - 1.0, 2.0 * c_one * d_one
    r_two, i_two = 2.0 * r_one * r_one - 1.0, 2.0 * r_one * i_one
    turn = 4.0 * r_two * r_two - 2.0
    before, now = r_two, r_two
    before_s, now_s = -i_two, i_two
    for n in range(4):
        put(4 + n, now)
        put(8 + n, now_s)
        before, now = now, turn * now - before
        before_s, now_s = now_s, turn * now_s - before_s
    put(12, phase_r)
    put(13, phase_i)


def swap_parts(value):
    return pltpu.roll(value, 4, 0)


def forward(tiles, lefts, tops, rests):
    found = [nn_dot(k, tile.reshape(64, 128)) for k, tile in zip(lefts, tiles)]
    pairs = []
    for left in found:
        r_up, r_lo, i_up, i_lo = left[0:16], left[16:32], left[32:48], left[48:64]
        left = jnp.concatenate(
            [
                jnp.concatenate([r_up + r_lo, i_lo - i_up], axis=0),
                jnp.concatenate([i_up + i_lo, r_up - r_lo], axis=0),
            ],
            axis=1,
        )
        pairs.append(split(left))
    large = [nn_dot(jnp.concatenate(pair, axis=0), m) for pair, m in zip(pairs, tops)]
    tiny = [nn_dot(pair[0], m) for pair, m in zip(pairs, rests)]
    return [(x[:32] + x[32:] + y).astype(BF) for x, y in zip(large, tiny)]


def backward(growns, lefts, tops, rests):
    pairs = [
        split(jnp.concatenate([grown[32 * r:32 * r + 32] for r in range(4)], axis=1)) for grown in growns
    ]
    large = [nt_dot(jnp.concatenate(pair, axis=0), m) for pair, m in zip(pairs, tops)]
    tiny = [nt_dot(pair[0], m) for pair, m in zip(pairs, rests)]
    halves = []
    for x, y in zip(large, tiny):
        back = x[:32] + x[32:] + y
        a_r, b_r, a_i, b_i = back[:16, :128], back[16:, :128], back[:16, 128:], back[16:, 128:]
        back = jnp.concatenate([a_r + b_i, a_r - b_i, a_i - b_r, a_i + b_r], axis=0)
        halves.append(jnp.concatenate(split(back), axis=1))
    parts = [nn_dot(k, half) for k, half in zip(lefts, halves)]
    return [(part[:, :128] + part[:, 128:]).astype(BF).reshape(2, 32, 128) for part in parts]


def block_kernel(order_ref, pos_ref, plane_ref, *refs):
    obs_ref, uv_ref, wgt_ref, tile_ref, left_ref, leftt_ref, right_ref = refs[:7]
    res_ref, out_ref, u_tab, v_tab, prod, grown, coef, vis, seen_buf, seen_sem = refs[-10:]
    width = 32
    step = pl.program_id(0)
    now = lax.rem(step, 2)

    def fetch(turn, side):
        for b in range(STEP):
            pltpu.make_async_copy(
                obs_ref.at[order_ref[turn * STEP + b]], seen_buf.at[side, b], seen_sem.at[side]
            ).start()

    @pl.when(step == 0)
    def _():
        fetch(0, 0)

    @pl.when(step + 1 < pl.num_programs(0))
    def _():
        fetch(step + 1, 1 - now)

    pltpu.make_async_copy(obs_ref.at[pl.ds(0, STEP)], seen_buf.at[now], seen_sem.at[now]).wait()
    tables(uv_ref, u_tab, v_tab, width)
    sign = jnp.where(lax.broadcasted_iota(jnp.int32, (8, CHUNK), 0) < 4, -1.0, 1.0).astype(F32)

    def matrices_of(blocks, own):
        planes = [plane_ref[step * STEP + b] for b in blocks]
        return (
            [own[plane] for plane in planes],
            [right_ref[plane, 0] for plane in planes],
            [right_ref[plane, 1] for plane in planes],
        )

    def first(blocks):
        tiles = [tile_ref[pos_ref[step * STEP + b]] for b in blocks]
        for b, found in zip(blocks, forward(tiles, *matrices_of(blocks, left_ref))):
            for r in range(4):
                coef[b, 32 * r:32 * r + 32, :] = found[:, 64 * r:64 * r + 64]

    def products(b):
        for start in range(0, 1024, CHUNK):
            lanes = slice(start, start + CHUNK)
            table = column(u_tab, b, start)
            for r in range(4):
                row = row_of(v_tab, r, b, start, width)
                prod[b, width * r:width * r + width, lanes] = (table * row).astype(BF)

    def middle(b):
        for start in range(0, 1024, CHUNK):
            lanes = slice(start, start + CHUNK)
            spread = tn_dot(coef[b], prod[b, :, lanes])
            rows = [row_of(v_tab, 4 + g, b, start, 8) for g in range(8)]
            total = spread[0:8] * rows[0]
            for g in range(1, 8):
                total = total + spread[8 * g:8 * g + 8] * rows[g]
            phase_r, phase_i = row_of(v_tab, 12, b, start, 8), row_of(v_tab, 13, b, start, 8) * sign
            total = total * phase_r + swap_parts(total) * phase_i
            seen = jnp.concatenate([seen_buf[now, b, 0, :, lanes], seen_buf[now, b, 1, :, lanes]], axis=0)
            resid = seen - total
            res_ref[b, :, lanes] = resid
            scaled = resid * jnp.broadcast_to(wgt_ref[b:b + 1, lanes], (8, CHUNK))
            turned = scaled * phase_r - swap_parts(scaled) * phase_i
            for g in range(0, 8, 2):
                pair = jnp.concatenate([turned * rows[g], turned * rows[g + 1]], axis=0)
                vis[b, 8 * g:8 * g + 16, lanes] = pair.astype(BF)
        grown[b] = nt_dot(prod[b], vis[b])

    def last(blocks):
        done = backward([grown[b] for b in blocks], *matrices_of(blocks, leftt_ref))
        for b, part in zip(blocks, done):
            out_ref[pos_ref[step * STEP + b]] = part

    first(list(range(STEP)))
    for b in range(STEP):
        products(b)
        middle(b)
    last(list(range(STEP)))


def plane_matrices(w_kernels):
    planes, _, width, _ = w_kernels.shape
    half = width // 2
    turned = jnp.concatenate([w_kernels[:, :, half:], w_kernels[:, :, half - 1::-1]], axis=2)
    kr, ki = turned[:, 0], turned[:, 1]
    left = jnp.concatenate([jnp.concatenate([kr, -ki], axis=2), jnp.concatenate([ki, kr], axis=2)], axis=1)
    mix = np.zeros((4, 8, width), np.complex64)
    for r in range(4):
        for g in range(8):
            for s1 in (1, -1):
                for s3 in (1, -1):
                    i, n = r % 2, g % 4
                    m1 = 4 + n if s1 > 0 else 3 - n
                    m2 = 2 + i if s3 > 0 else 1 - i
                    mix[r, g, 4 * m1 + m2] = (1j * s3 if r >= 2 else 1) * (1j * s1 if g >= 4 else 1)
    spread = np.zeros((2, width, 2, 4, 8, 2, 4), np.float32)
    for into in range(2):
        for outof in range(2):
            for src in range(2):
                unit = 1j if src else 1
                factor = mix * unit
                if into == 0 and outof == 0:
                    value = factor.real
                elif into == 0 and outof == 1:
                    value = factor.imag
                elif into == 1 and outof == 0:
                    value = -factor.imag
                else:
                    value = factor.real
                spread[src, :, into, :, :, outof, :] = value.transpose(2, 0, 1)[:, :, :, None]
    spread = spread.reshape(2, width, 512)
    grid = jnp.einsum("zcmk,cmq->zkq", w_kernels, jnp.asarray(spread, BF), preferred_element_type=F32)
    grid = grid * (1.0 / width)
    top = lax.reduce_precision(grid, 8, 7)
    grid = jnp.stack([top.astype(BF), (grid - top).astype(BF)], axis=1)
    grid = grid.reshape(planes, 2, width, 2, 256).transpose(0, 1, 3, 2, 4)
    pol = np.arange(256) % 4
    mask = (pol[None, :] == np.arange(4)[:, None])[None, None, None, :, None, :]
    right = jnp.where(jnp.asarray(mask), grid[:, :, :, None, :, :], jnp.zeros((), BF))
    right = right.reshape(planes, 2, 256, 256)
    return left, left.transpose(0, 2, 1), right


def degrid_grid(phase, order, position, planes, vis_obs, uv_coords, vis_weight, arrived, matrices, residual):
    blocks = vis_obs.shape[0]
    count = order.shape[0]
    left, leftt, right = matrices

    def whole(array):
        zeros = (0,) * array.ndim
        return pl.BlockSpec(array.shape, lambda i, *_: zeros, pipeline_mode=pl.Buffered(1))

    steps = count // STEP
    first = phase * steps
    operands = [vis_obs, uv_coords, vis_weight, arrived, left, leftt, right]
    in_specs = [
        pl.BlockSpec(memory_space=pl.ANY),
        pl.BlockSpec((2, STEP, 1024), lambda i, *_: (0, i + first, 0)),
        pl.BlockSpec((STEP, 1024), lambda i, *_: (i + first, 0)),
        whole(arrived),
        whole(left),
        whole(leftt),
        whole(right),
    ]
    aliases = {}
    if residual is not None:
        operands.append(residual)
        in_specs.append(pl.BlockSpec(memory_space=pl.ANY))
        aliases = {3 + len(operands) - 1: 0}
    return pl.pallas_call(
        block_kernel,
        grid_spec=pltpu.PrefetchScalarGridSpec(
            num_scalar_prefetch=3,
            grid=(steps,),
            in_specs=in_specs,
            out_specs=[
                pl.BlockSpec((STEP, 8, 1024), lambda i, *_: (i + first, 0, 0)),
                whole(arrived),
            ],
            scratch_shapes=[
                pltpu.VMEM((8, 32 * STEP, 128), F32),
                pltpu.VMEM((8, 16 * STEP, 128), F32),
                pltpu.VMEM((STEP, 128, 1024), BF),
                pltpu.VMEM((STEP, 128, 64), F32),
                pltpu.VMEM((STEP, 128, 64), BF),
                pltpu.VMEM((STEP, 64, 1024), BF),
                pltpu.VMEM((2, STEP, 2, 4, 1024), F32),
                pltpu.SemaphoreType.DMA((2,)),
            ],
        ),
        out_shape=[
            jax.ShapeDtypeStruct((blocks, 8, 1024), F32),
            jax.ShapeDtypeStruct(arrived.shape, BF),
        ],
        input_output_aliases=aliases,
        compiler_params=pltpu.CompilerParams(vmem_limit_bytes=63 << 20),
        cost_estimate=pl.CostEstimate(flops=count * 80_000_000, bytes_accessed=count * 120_000, transcendentals=0),
        name=f"degrid_grid_{phase}",
    )(order, position, planes, *operands)


def sum_kernel(slot_ref, scale_ref, part_ref, start_ref, out_ref, total):
    step = pl.program_id(0)
    count = part_ref.shape[0]

    @pl.when(step == 0)
    def _():
        total[...] = start_ref[...]

    def add(i, carry):
        slot = slot_ref[step * count + i]
        total[slot] = total[slot] + part_ref[i].astype(F32)
        return carry

    lax.fori_loop(0, count, add, 0, unroll=4)

    @pl.when(step == pl.num_programs(0) - 1)
    def _():
        out_ref[...] = total[: out_ref.shape[0]] * scale_ref[0]


def sum_slots(slots, scale, parts, start, rows):
    count = parts.shape[0] // 8
    shape = parts.shape[1:]
    return pl.pallas_call(
        sum_kernel,
        grid_spec=pltpu.PrefetchScalarGridSpec(
            num_scalar_prefetch=2,
            grid=(8,),
            in_specs=[
                pl.BlockSpec((count,) + shape, lambda i, *_: (i, 0, 0, 0)),
                pl.BlockSpec(start.shape, lambda i, *_: (0, 0, 0, 0), pipeline_mode=pl.Buffered(1)),
            ],
            out_specs=pl.BlockSpec((rows,) + shape, lambda i, *_: (0, 0, 0, 0), pipeline_mode=pl.Buffered(1)),
            scratch_shapes=[pltpu.VMEM(start.shape, F32)],
        ),
        out_shape=jax.ShapeDtypeStruct((rows,) + shape, F32),
        compiler_params=pltpu.CompilerParams(vmem_limit_bytes=63 << 20),
        cost_estimate=pl.CostEstimate(flops=4_000_000, bytes_accessed=6_000_000, transcendentals=0),
        name="sum_slots",
    )(slots, scale, parts, start)


def plan(target, blocks):
    same = target[:, None] == target[None, :]
    earlier = np.arange(blocks)[:, None] > np.arange(blocks)[None, :]
    rank = jnp.sum(same & earlier, axis=1, dtype=jnp.int32)
    double = jnp.sum(same, axis=1, dtype=jnp.int32) > 1
    singles = jnp.sum(earlier & ~double[None, :], axis=1, dtype=jnp.int32)
    spare = blocks // 2 - jnp.sum(double, dtype=jnp.int32) // 2
    phase = jnp.where(double, rank, (singles >= spare).astype(jnp.int32))
    return phase, earlier


def shards(vis_obs, uv_coords, vis_weight, block_group, tile_slot, w_plane, model_tiles, w_kernels):
    blocks, nvis = vis_weight.shape
    groups = lax.axis_size(AXES)
    owned = model_tiles.shape[0]
    half = blocks // 2
    target = block_group[:, 0]
    phase, earlier = plan(target, blocks)
    slot = jnp.arange(2 * groups, dtype=jnp.int32)
    wanted = jnp.max(
        jnp.where((target + phase * groups)[None, :] == slot[:, None], tile_slot[None, :], -1), axis=1
    ).reshape(2, groups)
    message = jnp.concatenate(
        [wanted.astype(F32).T, jnp.full((groups, 1), jnp.sum(vis_weight))], axis=1
    )
    message = lax.all_to_all(message, AXES, split_axis=0, concat_axis=0, tiled=True)
    requested = message[:, :2].astype(jnp.int32)
    scale = (blocks * groups * nvis) / jnp.sum(message[:, 2])

    def exchange(array):
        return lax.all_to_all(array, AXES, split_axis=0, concat_axis=0, tiled=True)

    chosen = [
        jnp.take(model_tiles, jnp.maximum(requested[:, turn], 0), axis=0, mode="clip")
        for turn in range(2)
    ]
    arrived = [exchange(chosen[0])]
    place = phase * half + jnp.sum(
        earlier & (phase[:, None] == phase[None, :]), axis=1, dtype=jnp.int32
    )
    at = place[None, :] == jnp.arange(blocks, dtype=jnp.int32)[:, None]

    def ordered(values):
        return jnp.sum(jnp.where(at, values[None, :], 0), axis=1, dtype=jnp.int32)

    order = ordered(jnp.arange(blocks, dtype=jnp.int32))
    position = ordered(target)
    planes = ordered(w_plane)
    uv_sorted = jnp.take(uv_coords.transpose(1, 0, 2), order, axis=1, mode="clip")
    weight_sorted = jnp.take(vis_weight, order, axis=0, mode="clip")
    matrices = plane_matrices(w_kernels)
    late, matrices, uv_sorted, weight_sorted, order, position, planes = lax.optimization_barrier(
        (chosen[1], matrices, uv_sorted, weight_sorted, order, position, planes)
    )
    arrived.append(exchange(late))
    residual = None
    returned = []
    for turn in range(2):
        part = slice(turn * half, turn * half + half)
        residual, outgoing = degrid_grid(
            turn, order[part], position[part], planes[part], vis_obs, uv_sorted, weight_sorted,
            arrived[turn], matrices, residual
        )
        returned.append(exchange(outgoing))
    residual = jnp.take(residual, place, axis=0, mode="clip").reshape(vis_obs.shape)
    slots = jnp.where(requested < 0, owned, requested)
    start = jnp.zeros((owned + 1,) + model_tiles.shape[1:], F32)
    one = jnp.ones((1,), F32)
    partial = sum_slots(slots[:, 0], one, returned[0], start, owned + 1)
    return residual, sum_slots(slots[:, 1], scale.reshape(1), returned[1], partial, owned)


def solution(mesh):
    return jax.shard_map(
        shards,
        mesh=mesh,
        in_specs=(
            P(AXES, None, None, None),
            P(AXES, None, None),
            P(AXES, None),
            P(AXES, None),
            P(AXES),
            P(AXES),
            P(AXES, None, None, None),
            P(),
        ),
        out_specs=(P(AXES, None, None, None), P(AXES, None, None, None)),
        check_vma=False,
    )
```

```python
import jax
import jax.numpy as jnp
import numpy as np
from jax import lax
from jax.experimental import pallas as pl
from jax.experimental.pallas import tpu as pltpu
from jax.sharding import PartitionSpec as P

AXES = ("facet", "vis")

BF = jnp.bfloat16
F32 = jnp.float32
STEP = 8
CHUNK = 256


def even_fit(func, terms):
    nodes = np.cos(np.pi * (np.arange(200) + 0.5) / 200) * 0.25
    squares = (nodes + 0.25) / 2
    powers = squares[:, None] ** np.arange(terms)[None, :]
    scale = powers.max(axis=0)
    solved = np.linalg.lstsq(powers / scale, func(np.sqrt(squares)), rcond=None)[0]
    return [float(value) for value in solved / scale]


COS_TERMS = even_fit(lambda t: np.cos(np.pi * t), 7)
SIN_TERMS = even_fit(lambda t: np.sin(np.pi * t) / t, 6)


def half_turn(t):
    square = t * t
    cosine = jnp.full_like(t, COS_TERMS[-1])
    for term in COS_TERMS[-2::-1]:
        cosine = cosine * square + term
    sine = jnp.full_like(t, SIN_TERMS[-1])
    for term in SIN_TERMS[-2::-1]:
        sine = sine * square + term
    return cosine, sine * t


def nt_dot(left, right):
    return lax.dot_general(left, right, (((1,), (1,)), ((), ())), preferred_element_type=F32)


def tn_dot(left, right):
    return lax.dot_general(left, right, (((0,), (0,)), ((), ())), preferred_element_type=F32)


def nn_dot(left, right):
    return jnp.dot(left, right, preferred_element_type=F32)


def lay(table, row, value):
    for t in range(value.shape[1] // 128):
        table[t, STEP * row:STEP * row + STEP, :] = value[:, 128 * t:128 * t + 128]


def column(table, b, start):
    pieces = [table[start // 128 + t, pl.ds(b, 32, stride=STEP), :] for t in range(CHUNK // 128)]
    return jnp.concatenate(pieces, axis=1)


def row_of(table, row, b, start, count):
    first = STEP * row + b
    pieces = [
        jnp.broadcast_to(table[start // 128 + t, first:first + 1, :], (count, 128))
        for t in range(CHUNK // 128)
    ]
    return jnp.concatenate(pieces, axis=1)


def split(value):
    top = value.astype(BF)
    return top, (value - top.astype(F32)).astype(BF)


def tables(uv_ref, u_tab, v_tab, width):
    scale = -1.0 / width
    a_one, b_one = half_turn(uv_ref[0] * scale)
    c_one, d_one = half_turn(uv_ref[1] * scale)
    phase_r = (a_one * c_one - b_one * d_one)
    phase_i = -a_one * d_one - b_one * c_one
    half = width // 2
    twice = 4.0 * a_one * a_one - 2.0
    before, now = a_one, a_one
    before_s, now_s = -b_one, b_one
    for j in range(half):
        lay(u_tab, j, now)
        lay(u_tab, half + j, now_s)
        before, now = now, twice * now - before
        before_s, now_s = now_s, twice * now_s - before_s

    def put(row, value):
        lay(v_tab, row, value)

    c_square = c_one * c_one
    turn = 4.0 * c_square - 2.0
    put(0, c_one)
    put(2, d_one)
    put(1, turn * c_one - c_one)
    put(3, turn * d_one + d_one)
    r_one, i_one = 2.0 * c_square - 1.0, 2.0 * c_one * d_one
    r_two, i_two = 2.0 * r_one * r_one - 1.0, 2.0 * r_one * i_one
    turn = 4.0 * r_two * r_two - 2.0
    before, now = r_two, r_two
    before_s, now_s = -i_two, i_two
    for n in range(4):
        put(4 + n, now)
        put(8 + n, now_s)
        before, now = now, turn * now - before
        before_s, now_s = now_s, turn * now_s - before_s
    put(12, phase_r)
    put(13, phase_i)


def swap_parts(value):
    return pltpu.roll(value, 4, 0)


def forward(tiles, lefts, tops, rests):
    found = [nn_dot(k, tile.reshape(64, 128)) for k, tile in zip(lefts, tiles)]
    pairs = []
    for left in found:
        r_up, r_lo, i_up, i_lo = left[0:16], left[16:32], left[32:48], left[48:64]
        left = jnp.concatenate(
            [
                jnp.concatenate([r_up + r_lo, i_lo - i_up], axis=0),
                jnp.concatenate([i_up + i_lo, r_up - r_lo], axis=0),
            ],
            axis=1,
        )
        pairs.append(split(left))
    large = [nn_dot(jnp.concatenate(pair, axis=0), m) for pair, m in zip(pairs, tops)]
    tiny = [nn_dot(pair[0], m) for pair, m in zip(pairs, rests)]
    return [(x[:32] + x[32:] + y).astype(BF) for x, y in zip(large, tiny)]


def backward(growns, lefts, tops, rests):
    pairs = [
        split(jnp.concatenate([grown[32 * r:32 * r + 32] for r in range(4)], axis=1)) for grown in growns
    ]
    large = [nt_dot(jnp.concatenate(pair, axis=0), m) for pair, m in zip(pairs, tops)]
    tiny = [nt_dot(pair[0], m) for pair, m in zip(pairs, rests)]
    halves = []
    for x, y in zip(large, tiny):
        back = x[:32] + x[32:] + y
        a_r, b_r, a_i, b_i = back[:16, :128], back[16:, :128], back[:16, 128:], back[16:, 128:]
        back = jnp.concatenate([a_r + b_i, a_r - b_i, a_i - b_r, a_i + b_r], axis=0)
        halves.append(jnp.concatenate(split(back), axis=1))
    parts = [nn_dot(k, half) for k, half in zip(lefts, halves)]
    return [(part[:, :128] + part[:, 128:]).astype(BF).reshape(2, 32, 128) for part in parts]


def block_kernel(order_ref, pos_ref, plane_ref, *refs):
    obs_ref, uv_ref, wgt_ref, tile_ref, left_ref, leftt_ref, right_ref = refs[:7]
    res_ref, out_ref, u_tab, v_tab, prod, grown, coef, vis, seen_buf, seen_sem = refs[-10:]
    width = 32
    step = pl.program_id(0)
    now = lax.rem(step, 2)

    def fetch(turn, side):
        for b in range(STEP):
            pltpu.make_async_copy(
                obs_ref.at[order_ref[turn * STEP + b]], seen_buf.at[side, b], seen_sem.at[side]
            ).start()

    @pl.when(step == 0)
    def _():
        fetch(0, 0)

    @pl.when(step + 1 < pl.num_programs(0))
    def _():
        fetch(step + 1, 1 - now)

    pltpu.make_async_copy(obs_ref.at[pl.ds(0, STEP)], seen_buf.at[now], seen_sem.at[now]).wait()
    tables(uv_ref, u_tab, v_tab, width)
    sign = jnp.where(lax.broadcasted_iota(jnp.int32, (8, CHUNK), 0) < 4, -1.0, 1.0).astype(F32)

    def matrices_of(blocks, own):
        planes = [plane_ref[step * STEP + b] for b in blocks]
        return (
            [own[plane] for plane in planes],
            [right_ref[plane, 0] for plane in planes],
            [right_ref[plane, 1] for plane in planes],
        )

    def first(blocks):
        tiles = [tile_ref[pos_ref[step * STEP + b]] for b in blocks]
        for b, found in zip(blocks, forward(tiles, *matrices_of(blocks, left_ref))):
            for r in range(4):
                coef[b, 32 * r:32 * r + 32, :] = found[:, 64 * r:64 * r + 64]

    def products(b):
        for start in range(0, 1024, CHUNK):
            lanes = slice(start, start + CHUNK)
            table = column(u_tab, b, start)
            for r in range(4):
                row = row_of(v_tab, r, b, start, width)
                prod[b, width * r:width * r + width, lanes] = (table * row).astype(BF)

    def middle(b):
        for start in range(0, 1024, CHUNK):
            lanes = slice(start, start + CHUNK)
            spread = tn_dot(coef[b], prod[b, :, lanes])
            rows = [row_of(v_tab, 4 + g, b, start, 8) for g in range(8)]
            total = spread[0:8] * rows[0]
            for g in range(1, 8):
                total = total + spread[8 * g:8 * g + 8] * rows[g]
            phase_r, phase_i = row_of(v_tab, 12, b, start, 8), row_of(v_tab, 13, b, start, 8) * sign
            total = total * phase_r + swap_parts(total) * phase_i
            seen = jnp.concatenate([seen_buf[now, b, 0, :, lanes], seen_buf[now, b, 1, :, lanes]], axis=0)
            resid = seen - total
            res_ref[b, :, lanes] = resid
            scaled = resid * jnp.broadcast_to(wgt_ref[b:b + 1, lanes], (8, CHUNK))
            turned = scaled * phase_r - swap_parts(scaled) * phase_i
            for g in range(0, 8, 2):
                pair = jnp.concatenate([turned * rows[g], turned * rows[g + 1]], axis=0)
                vis[b, 8 * g:8 * g + 16, lanes] = pair.astype(BF)
        grown[b] = nt_dot(prod[b], vis[b])

    def last(blocks):
        done = backward([grown[b] for b in blocks], *matrices_of(blocks, leftt_ref))
        for b, part in zip(blocks, done):
            out_ref[pos_ref[step * STEP + b]] = part

    first(list(range(STEP)))
    for b in range(STEP):
        products(b)
        middle(b)
    last(list(range(STEP)))


def plane_matrices(w_kernels):
    planes, _, width, _ = w_kernels.shape
    half = width // 2
    turned = jnp.concatenate([w_kernels[:, :, half:], w_kernels[:, :, half - 1::-1]], axis=2)
    kr, ki = turned[:, 0], turned[:, 1]
    left = jnp.concatenate([jnp.concatenate([kr, -ki], axis=2), jnp.concatenate([ki, kr], axis=2)], axis=1)
    mix = np.zeros((4, 8, width), np.complex64)
    for r in range(4):
        for g in range(8):
            for s1 in (1, -1):
                for s3 in (1, -1):
                    i, n = r % 2, g % 4
                    m1 = 4 + n if s1 > 0 else 3 - n
                    m2 = 2 + i if s3 > 0 else 1 - i
                    mix[r, g, 4 * m1 + m2] = (1j * s3 if r >= 2 else 1) * (1j * s1 if g >= 4 else 1)
    spread = np.zeros((2, width, 2, 4, 8, 2, 4), np.float32)
    for into in range(2):
        for outof in range(2):
            for src in range(2):
                unit = 1j if src else 1
                factor = mix * unit
                if into == 0 and outof == 0:
                    value = factor.real
                elif into == 0 and outof == 1:
                    value = factor.imag
                elif into == 1 and outof == 0:
                    value = -factor.imag
                else:
                    value = factor.real
                spread[src, :, into, :, :, outof, :] = value.transpose(2, 0, 1)[:, :, :, None]
    spread = spread.reshape(2, width, 512)
    grid = jnp.einsum("zcmk,cmq->zkq", w_kernels, jnp.asarray(spread, BF), preferred_element_type=F32)
    grid = grid * (1.0 / width)
    top = lax.reduce_precision(grid, 8, 7)
    grid = jnp.stack([top.astype(BF), (grid - top).astype(BF)], axis=1)
    grid = grid.reshape(planes, 2, width, 2, 256).transpose(0, 1, 3, 2, 4)
    pol = np.arange(256) % 4
    mask = (pol[None, :] == np.arange(4)[:, None])[None, None, None, :, None, :]
    right = jnp.where(jnp.asarray(mask), grid[:, :, :, None, :, :], jnp.zeros((), BF))
    right = right.reshape(planes, 2, 256, 256)
    return left, left.transpose(0, 2, 1), right


def degrid_grid(phase, order, position, planes, vis_obs, uv_coords, vis_weight, arrived, matrices, residual):
    blocks = vis_obs.shape[0]
    count = order.shape[0]
    left, leftt, right = matrices

    def whole(array):
        zeros = (0,) * array.ndim
        return pl.BlockSpec(array.shape, lambda i, *_: zeros, pipeline_mode=pl.Buffered(1))

    steps = count // STEP
    first = phase * steps
    operands = [vis_obs, uv_coords, vis_weight, arrived, left, leftt, right]
    in_specs = [
        pl.BlockSpec(memory_space=pl.ANY),
        pl.BlockSpec((2, STEP, 1024), lambda i, *_: (0, i + first, 0)),
        pl.BlockSpec((STEP, 1024), lambda i, *_: (i + first, 0)),
        whole(arrived),
        whole(left),
        whole(leftt),
        whole(right),
    ]
    aliases = {}
    if residual is not None:
        operands.append(residual)
        in_specs.append(pl.BlockSpec(memory_space=pl.ANY))
        aliases = {3 + len(operands) - 1: 0}
    return pl.pallas_call(
        block_kernel,
        grid_spec=pltpu.PrefetchScalarGridSpec(
            num_scalar_prefetch=3,
            grid=(steps,),
            in_specs=in_specs,
            out_specs=[
                pl.BlockSpec((STEP, 8, 1024), lambda i, *_: (i + first, 0, 0)),
                whole(arrived),
            ],
            scratch_shapes=[
                pltpu.VMEM((8, 32 * STEP, 128), F32),
                pltpu.VMEM((8, 16 * STEP, 128), F32),
                pltpu.VMEM((STEP, 128, 1024), BF),
                pltpu.VMEM((STEP, 128, 64), F32),
                pltpu.VMEM((STEP, 128, 64), BF),
                pltpu.VMEM((STEP, 64, 1024), BF),
                pltpu.VMEM((2, STEP, 2, 4, 1024), F32),
                pltpu.SemaphoreType.DMA((2,)),
            ],
        ),
        out_shape=[
            jax.ShapeDtypeStruct((blocks, 8, 1024), F32),
            jax.ShapeDtypeStruct(arrived.shape, BF),
        ],
        input_output_aliases=aliases,
        compiler_params=pltpu.CompilerParams(vmem_limit_bytes=63 << 20),
        cost_estimate=pl.CostEstimate(flops=count * 80_000_000, bytes_accessed=count * 120_000, transcendentals=0),
        name=f"degrid_grid_{phase}",
    )(order, position, planes, *operands)


def sum_kernel(slot_ref, scale_ref, part_ref, start_ref, out_ref, total):
    step = pl.program_id(0)
    count = part_ref.shape[0]

    @pl.when(step == 0)
    def _():
        total[...] = start_ref[...]

    def add(i, carry):
        slot = slot_ref[step * count + i]
        total[slot] = total[slot] + part_ref[i].astype(F32)
        return carry

    lax.fori_loop(0, count, add, 0, unroll=4)

    @pl.when(step == pl.num_programs(0) - 1)
    def _():
        out_ref[...] = total[: out_ref.shape[0]] * scale_ref[0]


def sum_slots(slots, scale, parts, start, rows):
    count = parts.shape[0] // 8
    shape = parts.shape[1:]
    return pl.pallas_call(
        sum_kernel,
        grid_spec=pltpu.PrefetchScalarGridSpec(
            num_scalar_prefetch=2,
            grid=(8,),
            in_specs=[
                pl.BlockSpec((count,) + shape, lambda i, *_: (i, 0, 0, 0)),
                pl.BlockSpec(start.shape, lambda i, *_: (0, 0, 0, 0), pipeline_mode=pl.Buffered(1)),
            ],
            out_specs=pl.BlockSpec((rows,) + shape, lambda i, *_: (0, 0, 0, 0), pipeline_mode=pl.Buffered(1)),
            scratch_shapes=[pltpu.VMEM(start.shape, F32)],
        ),
        out_shape=jax.ShapeDtypeStruct((rows,) + shape, F32),
        compiler_params=pltpu.CompilerParams(vmem_limit_bytes=63 << 20),
        cost_estimate=pl.CostEstimate(flops=4_000_000, bytes_accessed=6_000_000, transcendentals=0),
        name="sum_slots",
    )(slots, scale, parts, start)


def ask_kernel(column_ref, row_ref, weight_ref, message_out, plan_ref, ready, held, send_sem, recv_sem):
    blocks = row_ref.shape[1]
    facets, size = lax.axis_size("facet"), lax.axis_size("vis")
    groups = facets * size
    me = lax.axis_index("facet") * size + lax.axis_index("vis")
    barrier = pltpu.get_barrier_semaphore()

    def device(turn):
        peer = lax.rem(me + turn, groups)
        return peer, (peer // size, lax.rem(peer, size))

    def greet(turn, carry):
        pl.semaphore_signal(barrier, inc=1, device_id=device(turn)[1], device_id_type=pl.DeviceIdType.MESH)
        return carry

    lax.fori_loop(1, groups, greet, 0)

    square = (blocks, blocks)
    down = lax.broadcasted_iota(jnp.int32, square, 0)
    across = lax.broadcasted_iota(jnp.int32, square, 1)
    one, zero = jnp.ones(square, F32), jnp.zeros(square, F32)
    target_c, plane_c = column_ref[:, 0:1], column_ref[:, 1:2]
    target_r, slot_r = row_ref[0:1], row_ref[1:2]
    same = jnp.where(target_c == target_r, one, zero)
    before = jnp.where(down < across, one, zero)
    equal = jnp.where(down == across, one, zero)
    rank = jnp.sum(same * before, axis=0, keepdims=True)
    double_r = jnp.where(jnp.sum(same, axis=0, keepdims=True) > 1.5, 1.0, 0.0)
    single_c = jnp.where(jnp.sum(same, axis=1, keepdims=True) > 1.5, 0.0, 1.0)
    ahead = jnp.sum(before * single_c, axis=0, keepdims=True)
    spare = 0.5 * blocks - 0.5 * jnp.sum(double_r, axis=1, keepdims=True)
    phase_r = double_r * rank + (1.0 - double_r) * jnp.where(ahead > spare - 0.5, 1.0, 0.0)
    asked = []
    for turn in range(2):
        mine = (down == target_r) & (jnp.abs(phase_r - turn) < 0.5)
        asked.append(jnp.max(jnp.where(mine, slot_r.astype(F32), -1.0), axis=1, keepdims=True))
    weight = jnp.sum(jnp.sum(weight_ref[...], axis=0, keepdims=True), axis=1, keepdims=True)
    ready[...] = jnp.where(across == 0, asked[0], jnp.where(across == 1, asked[1], weight))

    phase_c = jnp.sum(equal * phase_r, axis=1, keepdims=True)
    alike = jnp.where(jnp.abs(phase_c - phase_r) < 0.5, one, zero)
    place_r = phase_r * (0.5 * blocks) + jnp.sum(before * alike, axis=0, keepdims=True)
    place_c = jnp.sum(equal * place_r, axis=1, keepdims=True)
    at = jnp.where(jnp.abs(place_c - across.astype(F32)) < 0.5, one, zero)
    rows = [
        place_r,
        jnp.sum(at * down.astype(F32), axis=0, keepdims=True),
        jnp.sum(at * target_c.astype(F32), axis=0, keepdims=True),
        jnp.sum(at * plane_c.astype(F32), axis=0, keepdims=True),
    ]
    plan_ref[...] = jnp.concatenate(rows + rows, axis=0).astype(jnp.int32)

    pl.semaphore_wait(barrier, groups - 1)

    def push(turn, carry):
        peer, where = device(turn)
        pltpu.make_async_remote_copy(
            src_ref=ready.at[pl.ds(peer, 1)],
            dst_ref=held.at[pl.ds(me, 1)],
            send_sem=send_sem,
            recv_sem=recv_sem,
            device_id=where,
            device_id_type=pl.DeviceIdType.MESH,
        ).start()
        return carry

    lax.fori_loop(1, groups, push, 0)
    everything = pltpu.make_async_remote_copy(
        src_ref=ready.at[pl.ds(0, groups - 1)],
        dst_ref=held.at[pl.ds(0, groups - 1)],
        send_sem=send_sem,
        recv_sem=recv_sem,
        device_id=device(1)[1],
        device_id_type=pl.DeviceIdType.MESH,
    )
    everything.wait_send()
    everything.wait_recv()
    message_out[...] = jnp.where(down == me, ready[...], held[...])


def ask(block_group, tile_slot, w_plane, vis_weight):
    blocks = tile_slot.shape[0]
    groups = lax.axis_size(AXES)
    columns = jnp.concatenate([block_group, w_plane[:, None]], axis=1)
    rows = jnp.stack([block_group[:, 0], tile_slot])
    return pl.pallas_call(
        ask_kernel,
        in_specs=[pl.BlockSpec(memory_space=pltpu.VMEM)] * 3,
        out_specs=[pl.BlockSpec(memory_space=pltpu.VMEM)] * 2,
        out_shape=[
            jax.ShapeDtypeStruct((groups, 128), F32),
            jax.ShapeDtypeStruct((8, blocks), jnp.int32),
        ],
        scratch_shapes=[
            pltpu.VMEM((groups, 128), F32),
            pltpu.VMEM((groups, 128), F32),
            pltpu.SemaphoreType.DMA,
            pltpu.SemaphoreType.DMA,
        ],
        compiler_params=pltpu.CompilerParams(collective_id=0, has_side_effects=True),
        name="ask",
    )(columns, rows, vis_weight)


def shards(vis_obs, uv_coords, vis_weight, block_group, tile_slot, w_plane, model_tiles, w_kernels):
    blocks, nvis = vis_weight.shape
    groups = lax.axis_size(AXES)
    owned = model_tiles.shape[0]
    half = blocks // 2
    message, plan = ask(block_group, tile_slot, w_plane, vis_weight)
    place, order, position, planes = plan[0], plan[1], plan[2], plan[3]
    requested = message[:, :2].astype(jnp.int32)
    scale = (blocks * groups * nvis) / jnp.sum(message[:, 2])

    def exchange(array):
        return lax.all_to_all(array, AXES, split_axis=0, concat_axis=0, tiled=True)

    chosen = [
        jnp.take(model_tiles, jnp.maximum(requested[:, turn], 0), axis=0, mode="clip")
        for turn in range(2)
    ]
    arrived = [exchange(chosen[0])]
    uv_sorted = jnp.take(uv_coords.transpose(1, 0, 2), order, axis=1, mode="clip")
    weight_sorted = jnp.take(vis_weight, order, axis=0, mode="clip")
    matrices = plane_matrices(w_kernels)
    late, matrices, uv_sorted, weight_sorted, order, position, planes = lax.optimization_barrier(
        (chosen[1], matrices, uv_sorted, weight_sorted, order, position, planes)
    )
    arrived.append(exchange(late))
    residual = None
    returned = []
    for turn in range(2):
        part = slice(turn * half, turn * half + half)
        residual, outgoing = degrid_grid(
            turn, order[part], position[part], planes[part], vis_obs, uv_sorted, weight_sorted,
            arrived[turn], matrices, residual
        )
        returned.append(exchange(outgoing))
    residual = jnp.take(residual, place, axis=0, mode="clip").reshape(vis_obs.shape)
    slots = jnp.where(requested < 0, owned, requested)
    start = jnp.zeros((owned + 1,) + model_tiles.shape[1:], F32)
    one = jnp.ones((1,), F32)
    partial = sum_slots(slots[:, 0], one, returned[0], start, owned + 1)
    return residual, sum_slots(slots[:, 1], scale.reshape(1), returned[1], partial, owned)


def solution(mesh):
    return jax.shard_map(
        shards,
        mesh=mesh,
        in_specs=(
            P(AXES, None, None, None),
            P(AXES, None, None),
            P(AXES, None),
            P(AXES, None),
            P(AXES),
            P(AXES),
            P(AXES, None, None, None),
            P(),
        ),
        out_specs=(P(AXES, None, None, None), P(AXES, None, None, None)),
        check_vma=False,
    )
```

```python
import jax
import jax.numpy as jnp
import numpy as np
from jax import lax
from jax.experimental import pallas as pl
from jax.experimental.pallas import tpu as pltpu
from jax.sharding import PartitionSpec as P

AXES = ("facet", "vis")

BF = jnp.bfloat16
F32 = jnp.float32
STEP = 8
CHUNK = 512


def even_fit(func, terms):
    nodes = np.cos(np.pi * (np.arange(200) + 0.5) / 200) * 0.25
    squares = (nodes + 0.25) / 2
    powers = squares[:, None] ** np.arange(terms)[None, :]
    scale = powers.max(axis=0)
    solved = np.linalg.lstsq(powers / scale, func(np.sqrt(squares)), rcond=None)[0]
    return [float(value) for value in solved / scale]


COS_TERMS = even_fit(lambda t: np.cos(np.pi * t), 7)
SIN_TERMS = even_fit(lambda t: np.sin(np.pi * t) / t, 6)


def half_turn(t):
    square = t * t
    cosine = jnp.full_like(t, COS_TERMS[-1])
    for term in COS_TERMS[-2::-1]:
        cosine = cosine * square + term
    sine = jnp.full_like(t, SIN_TERMS[-1])
    for term in SIN_TERMS[-2::-1]:
        sine = sine * square + term
    return cosine, sine * t


def nt_dot(left, right):
    return lax.dot_general(left, right, (((1,), (1,)), ((), ())), preferred_element_type=F32)


def tn_dot(left, right):
    return lax.dot_general(left, right, (((0,), (0,)), ((), ())), preferred_element_type=F32)


def nn_dot(left, right):
    return jnp.dot(left, right, preferred_element_type=F32)


def lay(table, row, value):
    for t in range(value.shape[1] // 128):
        table[t, STEP * row:STEP * row + STEP, :] = value[:, 128 * t:128 * t + 128]


def column(table, b, start):
    pieces = [table[start // 128 + t, pl.ds(b, 32, stride=STEP), :] for t in range(CHUNK // 128)]
    return jnp.concatenate(pieces, axis=1)


def row_of(table, row, b, start, count):
    first = STEP * row + b
    pieces = [
        jnp.broadcast_to(table[start // 128 + t, first:first + 1, :], (count, 128))
        for t in range(CHUNK // 128)
    ]
    return jnp.concatenate(pieces, axis=1)


def split(value):
    top = value.astype(BF)
    return top, (value - top.astype(F32)).astype(BF)


def tables(uv_ref, u_tab, v_tab, width):
    scale = -1.0 / width
    a_one, b_one = half_turn(uv_ref[0] * scale)
    c_one, d_one = half_turn(uv_ref[1] * scale)
    phase_r = (a_one * c_one - b_one * d_one)
    phase_i = -a_one * d_one - b_one * c_one
    half = width // 2
    twice = 4.0 * a_one * a_one - 2.0
    before, now = a_one, a_one
    before_s, now_s = -b_one, b_one
    for j in range(half):
        lay(u_tab, j, now)
        lay(u_tab, half + j, now_s)
        before, now = now, twice * now - before
        before_s, now_s = now_s, twice * now_s - before_s

    def put(row, value):
        lay(v_tab, row, value)

    c_square = c_one * c_one
    turn = 4.0 * c_square - 2.0
    put(0, c_one)
    put(2, d_one)
    put(1, turn * c_one - c_one)
    put(3, turn * d_one + d_one)
    r_one, i_one = 2.0 * c_square - 1.0, 2.0 * c_one * d_one
    r_two, i_two = 2.0 * r_one * r_one - 1.0, 2.0 * r_one * i_one
    turn = 4.0 * r_two * r_two - 2.0
    before, now = r_two, r_two
    before_s, now_s = -i_two, i_two
    for n in range(4):
        put(4 + n, now)
        put(8 + n, now_s)
        before, now = now, turn * now - before
        before_s, now_s = now_s, turn * now_s - before_s
    put(12, phase_r)
    put(13, phase_i)


def swap_parts(value):
    return pltpu.roll(value, 4, 0)


def forward(tiles, lefts, tops, rests):
    found = [nn_dot(k, tile.reshape(64, 128)) for k, tile in zip(lefts, tiles)]
    pairs = []
    for left in found:
        r_up, r_lo, i_up, i_lo = left[0:16], left[16:32], left[32:48], left[48:64]
        left = jnp.concatenate(
            [
                jnp.concatenate([r_up + r_lo, i_lo - i_up], axis=0),
                jnp.concatenate([i_up + i_lo, r_up - r_lo], axis=0),
            ],
            axis=1,
        )
        pairs.append(split(left))
    large = [nn_dot(jnp.concatenate(pair, axis=0), m) for pair, m in zip(pairs, tops)]
    return [(x[:32] + x[32:]).astype(BF) for x in large]


def backward(growns, lefts, tops, rests):
    pairs = [
        split(jnp.concatenate([grown[32 * r:32 * r + 32] for r in range(4)], axis=1)) for grown in growns
    ]
    large = [nt_dot(jnp.concatenate(pair, axis=0), m) for pair, m in zip(pairs, tops)]
    tiny = [nt_dot(pair[0], m) for pair, m in zip(pairs, rests)]
    halves = []
    for x, y in zip(large, tiny):
        back = x[:32] + x[32:] + y
        a_r, b_r, a_i, b_i = back[:16, :128], back[16:, :128], back[:16, 128:], back[16:, 128:]
        back = jnp.concatenate([a_r + b_i, a_r - b_i, a_i - b_r, a_i + b_r], axis=0)
        halves.append(jnp.concatenate(split(back), axis=1))
    parts = [nn_dot(k, half) for k, half in zip(lefts, halves)]
    return [(part[:, :128] + part[:, 128:]).astype(BF).reshape(2, 32, 128) for part in parts]


def block_kernel(order_ref, pos_ref, plane_ref, *refs):
    obs_ref, uv_ref, wgt_ref, tile_ref, left_ref, leftt_ref, right_ref = refs[:7]
    res_ref, out_ref, u_tab, v_tab, prod, grown, coef, vis, seen_buf, seen_sem = refs[-10:]
    width = 32
    step = pl.program_id(0)
    now = lax.rem(step, 2)

    def fetch(turn, side):
        for b in range(STEP):
            pltpu.make_async_copy(
                obs_ref.at[order_ref[turn * STEP + b]], seen_buf.at[side, b], seen_sem.at[side]
            ).start()

    @pl.when(step == 0)
    def _():
        fetch(0, 0)

    @pl.when(step + 1 < pl.num_programs(0))
    def _():
        fetch(step + 1, 1 - now)

    pltpu.make_async_copy(obs_ref.at[pl.ds(0, STEP)], seen_buf.at[now], seen_sem.at[now]).wait()
    tables(uv_ref, u_tab, v_tab, width)
    sign = jnp.where(lax.broadcasted_iota(jnp.int32, (8, CHUNK), 0) < 4, -1.0, 1.0).astype(F32)

    def matrices_of(blocks, own):
        planes = [plane_ref[step * STEP + b] for b in blocks]
        return (
            [own[plane] for plane in planes],
            [right_ref[plane, 0] for plane in planes],
            [right_ref[plane, 1] for plane in planes],
        )

    def first(blocks):
        tiles = [tile_ref[pos_ref[step * STEP + b]] for b in blocks]
        for b, found in zip(blocks, forward(tiles, *matrices_of(blocks, left_ref))):
            for r in range(4):
                coef[b, 32 * r:32 * r + 32, :] = found[:, 64 * r:64 * r + 64]

    def products(b):
        for start in range(0, 1024, CHUNK):
            lanes = slice(start, start + CHUNK)
            table = column(u_tab, b, start)
            for r in range(4):
                row = row_of(v_tab, r, b, start, width)
                prod[b, width * r:width * r + width, lanes] = (table * row).astype(BF)

    def middle(b):
        for start in range(0, 1024, CHUNK):
            lanes = slice(start, start + CHUNK)
            spread = tn_dot(coef[b], prod[b, :, lanes])
            rows = [row_of(v_tab, 4 + g, b, start, 8) for g in range(8)]
            total = spread[0:8] * rows[0]
            for g in range(1, 8):
                total = total + spread[8 * g:8 * g + 8] * rows[g]
            phase_r, phase_i = row_of(v_tab, 12, b, start, 8), row_of(v_tab, 13, b, start, 8) * sign
            total = total * phase_r + swap_parts(total) * phase_i
            seen = jnp.concatenate([seen_buf[now, b, 0, :, lanes], seen_buf[now, b, 1, :, lanes]], axis=0)
            resid = seen - total
            res_ref[b, :, lanes] = resid
            scaled = resid * jnp.broadcast_to(wgt_ref[b:b + 1, lanes], (8, CHUNK))
            turned = scaled * phase_r - swap_parts(scaled) * phase_i
            for g in range(0, 8, 2):
                pair = jnp.concatenate([turned * rows[g], turned * rows[g + 1]], axis=0)
                vis[b, 8 * g:8 * g + 16, lanes] = pair.astype(BF)
        grown[b] = nt_dot(prod[b], vis[b])

    def last(blocks):
        done = backward([grown[b] for b in blocks], *matrices_of(blocks, leftt_ref))
        for b, part in zip(blocks, done):
            out_ref[pos_ref[step * STEP + b]] = part

    first(list(range(STEP)))
    for b in range(STEP):
        products(b)
        middle(b)
    last(list(range(STEP)))


def plane_matrices(w_kernels):
    planes, _, width, _ = w_kernels.shape
    half = width // 2
    turned = jnp.concatenate([w_kernels[:, :, half:], w_kernels[:, :, half - 1::-1]], axis=2)
    kr, ki = turned[:, 0], turned[:, 1]
    left = jnp.concatenate([jnp.concatenate([kr, -ki], axis=2), jnp.concatenate([ki, kr], axis=2)], axis=1)
    mix = np.zeros((4, 8, width), np.complex64)
    for r in range(4):
        for g in range(8):
            for s1 in (1, -1):
                for s3 in (1, -1):
                    i, n = r % 2, g % 4
                    m1 = 4 + n if s1 > 0 else 3 - n
                    m2 = 2 + i if s3 > 0 else 1 - i
                    mix[r, g, 4 * m1 + m2] = (1j * s3 if r >= 2 else 1) * (1j * s1 if g >= 4 else 1)
    spread = np.zeros((2, width, 2, 4, 8, 2, 4), np.float32)
    for into in range(2):
        for outof in range(2):
            for src in range(2):
                unit = 1j if src else 1
                factor = mix * unit
                if into == 0 and outof == 0:
                    value = factor.real
                elif into == 0 and outof == 1:
                    value = factor.imag
                elif into == 1 and outof == 0:
                    value = -factor.imag
                else:
                    value = factor.real
                spread[src, :, into, :, :, outof, :] = value.transpose(2, 0, 1)[:, :, :, None]
    spread = spread.reshape(2, width, 512)
    grid = jnp.einsum("zcmk,cmq->zkq", w_kernels, jnp.asarray(spread, BF), preferred_element_type=F32)
    grid = grid * (1.0 / width)
    top = lax.reduce_precision(grid, 8, 7)
    grid = jnp.stack([top.astype(BF), (grid - top).astype(BF)], axis=1)
    grid = grid.reshape(planes, 2, width, 2, 256).transpose(0, 1, 3, 2, 4)
    pol = np.arange(256) % 4
    mask = (pol[None, :] == np.arange(4)[:, None])[None, None, None, :, None, :]
    right = jnp.where(jnp.asarray(mask), grid[:, :, :, None, :, :], jnp.zeros((), BF))
    right = right.reshape(planes, 2, 256, 256)
    return left, left.transpose(0, 2, 1), right


def degrid_grid(phase, order, position, planes, vis_obs, uv_coords, vis_weight, arrived, matrices, residual):
    blocks = vis_obs.shape[0]
    count = order.shape[0]
    left, leftt, right = matrices

    def whole(array):
        zeros = (0,) * array.ndim
        return pl.BlockSpec(array.shape, lambda i, *_: zeros, pipeline_mode=pl.Buffered(1))

    steps = count // STEP
    first = phase * steps
    operands = [vis_obs, uv_coords, vis_weight, arrived, left, leftt, right]
    in_specs = [
        pl.BlockSpec(memory_space=pl.ANY),
        pl.BlockSpec((2, STEP, 1024), lambda i, *_: (0, i + first, 0)),
        pl.BlockSpec((STEP, 1024), lambda i, *_: (i + first, 0)),
        whole(arrived),
        whole(left),
        whole(leftt),
        whole(right),
    ]
    aliases = {}
    if residual is not None:
        operands.append(residual)
        in_specs.append(pl.BlockSpec(memory_space=pl.ANY))
        aliases = {3 + len(operands) - 1: 0}
    return pl.pallas_call(
        block_kernel,
        grid_spec=pltpu.PrefetchScalarGridSpec(
            num_scalar_prefetch=3,
            grid=(steps,),
            in_specs=in_specs,
            out_specs=[
                pl.BlockSpec((STEP, 8, 1024), lambda i, *_: (i + first, 0, 0)),
                whole(arrived),
            ],
            scratch_shapes=[
                pltpu.VMEM((8, 32 * STEP, 128), F32),
                pltpu.VMEM((8, 16 * STEP, 128), F32),
                pltpu.VMEM((STEP, 128, 1024), BF),
                pltpu.VMEM((STEP, 128, 64), F32),
                pltpu.VMEM((STEP, 128, 64), BF),
                pltpu.VMEM((STEP, 64, 1024), BF),
                pltpu.VMEM((2, STEP, 2, 4, 1024), F32),
                pltpu.SemaphoreType.DMA((2,)),
            ],
        ),
        out_shape=[
            jax.ShapeDtypeStruct((blocks, 8, 1024), F32),
            jax.ShapeDtypeStruct(arrived.shape, BF),
        ],
        input_output_aliases=aliases,
        compiler_params=pltpu.CompilerParams(vmem_limit_bytes=63 << 20),
        cost_estimate=pl.CostEstimate(flops=count * 80_000_000, bytes_accessed=count * 120_000, transcendentals=0),
        name=f"degrid_grid_{phase}",
    )(order, position, planes, *operands)


def sum_kernel(slot_ref, part_ref, start_ref, out_ref):
    step = pl.program_id(0)
    count = part_ref.shape[0]

    @pl.when(step == 0)
    def _():
        out_ref[...] = start_ref[...]

    def add(i, carry):
        slot = slot_ref[step * count + i]
        part = jnp.where(slot >= 0, part_ref[i].astype(F32), 0.0)
        row = jnp.maximum(slot, 0)
        out_ref[row] = out_ref[row] + part
        return carry

    lax.fori_loop(0, count, add, 0, unroll=8)


def sum_slots(slots, parts, start):
    steps = 2
    count = parts.shape[0] // steps
    shape = parts.shape[1:]

    def whole():
        return pl.BlockSpec(start.shape, lambda i, *_: (0, 0, 0, 0), pipeline_mode=pl.Buffered(1))

    return pl.pallas_call(
        sum_kernel,
        grid_spec=pltpu.PrefetchScalarGridSpec(
            num_scalar_prefetch=1,
            grid=(steps,),
            in_specs=[pl.BlockSpec((count,) + shape, lambda i, *_: (i, 0, 0, 0)), whole()],
            out_specs=whole(),
        ),
        out_shape=jax.ShapeDtypeStruct(start.shape, F32),
        compiler_params=pltpu.CompilerParams(vmem_limit_bytes=63 << 20),
        cost_estimate=pl.CostEstimate(flops=4_000_000, bytes_accessed=6_000_000, transcendentals=0),
        name="sum_slots",
    )(slots, parts, start)


def ask_kernel(target_ref, slot_ref, plane_ref, weight_ref, message_out, sorted_ref, ready, held, send_sem, recv_sem):
    blocks = target_ref.shape[1]
    facets, size = lax.axis_size("facet"), lax.axis_size("vis")
    groups = facets * size
    me = lax.axis_index("facet") * size + lax.axis_index("vis")
    barrier = pltpu.get_barrier_semaphore()

    def device(turn):
        peer = lax.rem(me + turn, groups)
        return peer, (peer // size, lax.rem(peer, size))

    def greet(turn, carry):
        pl.semaphore_signal(barrier, inc=1, device_id=device(turn)[1], device_id_type=pl.DeviceIdType.MESH)
        return carry

    lax.fori_loop(1, groups, greet, 0)

    square = (blocks, blocks)
    down = lax.broadcasted_iota(jnp.int32, square, 0)
    across = lax.broadcasted_iota(jnp.int32, square, 1)
    one, zero = jnp.ones(square, F32), jnp.zeros(square, F32)
    before = jnp.where(down < across, one, zero)
    equal = jnp.where(down == across, one, zero)

    def turned(row):
        return jnp.sum(equal * row, axis=1, keepdims=True)

    target_r, slot_r = target_ref[...].astype(F32), slot_ref[...].astype(F32)
    target_c, plane_c = turned(target_r), turned(plane_ref[...].astype(F32))
    same = jnp.where(jnp.abs(target_c - target_r) < 0.5, one, zero)
    rank = jnp.sum(same * before, axis=0, keepdims=True)
    double_r = jnp.where(jnp.sum(same, axis=0, keepdims=True) > 1.5, 1.0, 0.0)
    single_c = jnp.where(jnp.sum(same, axis=1, keepdims=True) > 1.5, 0.0, 1.0)
    ahead = jnp.sum(before * single_c, axis=0, keepdims=True)
    spare = 0.5 * blocks - 0.5 * jnp.sum(double_r, axis=1, keepdims=True)
    phase_r = double_r * rank + (1.0 - double_r) * jnp.where(ahead > spare - 0.5, 1.0, 0.0)
    asked = []
    for turn in range(2):
        mine = (jnp.abs(down.astype(F32) - target_r) < 0.5) & (jnp.abs(phase_r - turn) < 0.5)
        asked.append(jnp.max(jnp.where(mine, slot_r, -1.0), axis=1, keepdims=True))
    weight = jnp.sum(jnp.sum(weight_ref[...], axis=0, keepdims=True), axis=1, keepdims=True)
    ready[...] = jnp.where(across == 0, asked[0], jnp.where(across == 1, asked[1], weight))

    phase_c = turned(phase_r)
    alike = jnp.where(jnp.abs(phase_c - phase_r) < 0.5, one, zero)
    place_r = phase_r * (0.5 * blocks) + jnp.sum(before * alike, axis=0, keepdims=True)
    place_c = turned(place_r)
    at = jnp.where(jnp.abs(place_c - across.astype(F32)) < 0.5, one, zero)
    rows = [
        place_r,
        jnp.sum(at * down.astype(F32), axis=0, keepdims=True),
        jnp.sum(at * target_c, axis=0, keepdims=True),
        jnp.sum(at * plane_c, axis=0, keepdims=True),
    ]
    sorted_ref[...] = jnp.concatenate(rows + rows, axis=0).astype(jnp.int32)

    pl.semaphore_wait(barrier, groups - 1)

    def push(turn, carry):
        peer, where = device(turn)
        pltpu.make_async_remote_copy(
            src_ref=ready.at[pl.ds(peer, 1)],
            dst_ref=held.at[pl.ds(me, 1)],
            send_sem=send_sem,
            recv_sem=recv_sem,
            device_id=where,
            device_id_type=pl.DeviceIdType.MESH,
        ).start()
        return carry

    lax.fori_loop(1, groups, push, 0)
    everything = pltpu.make_async_remote_copy(
        src_ref=ready.at[pl.ds(0, groups - 1)],
        dst_ref=held.at[pl.ds(0, groups - 1)],
        send_sem=send_sem,
        recv_sem=recv_sem,
        device_id=device(1)[1],
        device_id_type=pl.DeviceIdType.MESH,
    )
    everything.wait_send()
    everything.wait_recv()
    message_out[...] = jnp.where(down == me, ready[...], held[...])


def ask(block_group, tile_slot, w_plane, vis_weight):
    blocks = tile_slot.shape[0]
    groups = lax.axis_size(AXES)
    rows = [array.reshape(1, blocks) for array in (block_group, tile_slot, w_plane)]
    return pl.pallas_call(
        ask_kernel,
        in_specs=[pl.BlockSpec(memory_space=pltpu.VMEM)] * 4,
        out_specs=[pl.BlockSpec(memory_space=pltpu.VMEM)] * 2,
        out_shape=[
            jax.ShapeDtypeStruct((groups, 128), F32),
            jax.ShapeDtypeStruct((8, blocks), jnp.int32),
        ],
        scratch_shapes=[
            pltpu.VMEM((groups, 128), F32),
            pltpu.VMEM((groups, 128), F32),
            pltpu.SemaphoreType.DMA,
            pltpu.SemaphoreType.DMA,
        ],
        compiler_params=pltpu.CompilerParams(collective_id=0, has_side_effects=True),
        name="ask",
    )(*rows, vis_weight)


def shards(vis_obs, uv_coords, vis_weight, block_group, tile_slot, w_plane, model_tiles, w_kernels):
    blocks, nvis = vis_weight.shape
    groups = lax.axis_size(AXES)
    half = blocks // 2
    message, plan = ask(block_group, tile_slot, w_plane, vis_weight)
    place, order, position, planes = plan[0], plan[1], plan[2], plan[3]
    requested = message[:, :2].astype(jnp.int32)
    scale = (blocks * groups * nvis) / jnp.sum(message[:, 2])

    def exchange(array):
        return lax.all_to_all(array, AXES, split_axis=0, concat_axis=0, tiled=True)

    chosen = [
        jnp.take(model_tiles, jnp.maximum(requested[:, turn], 0), axis=0, mode="clip")
        for turn in range(2)
    ]
    arrived = [exchange(chosen[0])]
    uv_sorted = jnp.take(uv_coords.transpose(1, 0, 2), order, axis=1, mode="clip")
    weight_sorted = jnp.take(vis_weight, order, axis=0, mode="clip") * scale
    matrices = plane_matrices(w_kernels)
    late, matrices, uv_sorted, weight_sorted, order, position, planes = lax.optimization_barrier(
        (chosen[1], matrices, uv_sorted, weight_sorted, order, position, planes)
    )
    arrived.append(exchange(late))
    residual = None
    returned = []
    for turn in range(2):
        part = slice(turn * half, turn * half + half)
        residual, outgoing = degrid_grid(
            turn, order[part], position[part], planes[part], vis_obs, uv_sorted, weight_sorted,
            arrived[turn], matrices, residual
        )
        returned.append(exchange(outgoing))
    residual = jnp.take(residual, place, axis=0, mode="clip").reshape(vis_obs.shape)
    partial = sum_slots(requested[:, 0], returned[0], jnp.zeros(model_tiles.shape, F32))
    return residual, sum_slots(requested[:, 1], returned[1], partial)


def solution(mesh):
    return jax.shard_map(
        shards,
        mesh=mesh,
        in_specs=(
            P(AXES, None, None, None),
            P(AXES, None, None),
            P(AXES, None),
            P(AXES, None),
            P(AXES),
            P(AXES),
            P(AXES, None, None, None),
            P(),
        ),
        out_specs=(P(AXES, None, None, None), P(AXES, None, None, None)),
        check_vma=False,
    )
```

```python
import jax
import jax.numpy as jnp
import numpy as np
from jax import lax
from jax.experimental import pallas as pl
from jax.experimental.pallas import tpu as pltpu
from jax.sharding import PartitionSpec as P

AXES = ("facet", "vis")

BF = jnp.bfloat16
F32 = jnp.float32
STEP = 8
CHUNK = 512


def even_fit(func, terms):
    nodes = np.cos(np.pi * (np.arange(200) + 0.5) / 200) * 0.25
    squares = (nodes + 0.25) / 2
    powers = squares[:, None] ** np.arange(terms)[None, :]
    scale = powers.max(axis=0)
    solved = np.linalg.lstsq(powers / scale, func(np.sqrt(squares)), rcond=None)[0]
    return [float(value) for value in solved / scale]


COS_TERMS = even_fit(lambda t: np.cos(np.pi * t), 7)
SIN_TERMS = even_fit(lambda t: np.sin(np.pi * t) / t, 6)


def half_turn(t):
    square = t * t
    cosine = jnp.full_like(t, COS_TERMS[-1])
    for term in COS_TERMS[-2::-1]:
        cosine = cosine * square + term
    sine = jnp.full_like(t, SIN_TERMS[-1])
    for term in SIN_TERMS[-2::-1]:
        sine = sine * square + term
    return cosine, sine * t


def nt_dot(left, right):
    return lax.dot_general(left, right, (((1,), (1,)), ((), ())), preferred_element_type=F32)


def tn_dot(left, right):
    return lax.dot_general(left, right, (((0,), (0,)), ((), ())), preferred_element_type=F32)


def nn_dot(left, right):
    return jnp.dot(left, right, preferred_element_type=F32)


def lay(table, row, value):
    for t in range(value.shape[1] // 128):
        table[t, STEP * row:STEP * row + STEP, :] = value[:, 128 * t:128 * t + 128]


def column(table, b, start):
    pieces = [table[start // 128 + t, pl.ds(b, 32, stride=STEP), :] for t in range(CHUNK // 128)]
    return jnp.concatenate(pieces, axis=1)


def row_of(table, row, b, start, count):
    first = STEP * row + b
    pieces = [
        jnp.broadcast_to(table[start // 128 + t, first:first + 1, :], (count, 128))
        for t in range(CHUNK // 128)
    ]
    return jnp.concatenate(pieces, axis=1)


def split(value):
    top = value.astype(BF)
    return top, (value - top.astype(F32)).astype(BF)


def tables(uv_ref, u_tab, v_tab, width):
    scale = -1.0 / width
    a_one, b_one = half_turn(uv_ref[0] * scale)
    c_one, d_one = half_turn(uv_ref[1] * scale)
    phase_r = (a_one * c_one - b_one * d_one)
    phase_i = -a_one * d_one - b_one * c_one
    half = width // 2
    twice = 4.0 * a_one * a_one - 2.0
    before, now = a_one, a_one
    before_s, now_s = -b_one, b_one
    for j in range(half):
        lay(u_tab, j, now)
        lay(u_tab, half + j, now_s)
        before, now = now, twice * now - before
        before_s, now_s = now_s, twice * now_s - before_s

    def put(row, value):
        lay(v_tab, row, value)

    c_square = c_one * c_one
    turn = 4.0 * c_square - 2.0
    put(0, c_one)
    put(2, d_one)
    put(1, turn * c_one - c_one)
    put(3, turn * d_one + d_one)
    r_one, i_one = 2.0 * c_square - 1.0, 2.0 * c_one * d_one
    r_two, i_two = 2.0 * r_one * r_one - 1.0, 2.0 * r_one * i_one
    turn = 4.0 * r_two * r_two - 2.0
    before, now = r_two, r_two
    before_s, now_s = -i_two, i_two
    for n in range(4):
        put(4 + n, now)
        put(8 + n, now_s)
        before, now = now, turn * now - before
        before_s, now_s = now_s, turn * now_s - before_s
    put(12, phase_r)
    put(13, phase_i)


def swap_parts(value):
    return pltpu.roll(value, 4, 0)


def forward(tiles, lefts, tops, rests):
    found = [nn_dot(k, tile.reshape(64, 128)) for k, tile in zip(lefts, tiles)]
    pairs = []
    for left in found:
        r_up, r_lo, i_up, i_lo = left[0:16], left[16:32], left[32:48], left[48:64]
        left = jnp.concatenate(
            [
                jnp.concatenate([r_up + r_lo, i_lo - i_up], axis=0),
                jnp.concatenate([i_up + i_lo, r_up - r_lo], axis=0),
            ],
            axis=1,
        )
        pairs.append(split(left))
    large = [nn_dot(jnp.concatenate(pair, axis=0), m) for pair, m in zip(pairs, tops)]
    return [(x[:32] + x[32:]).astype(BF) for x in large]


def backward(growns, lefts, tops, rests):
    pairs = [
        split(jnp.concatenate([grown[32 * r:32 * r + 32] for r in range(4)], axis=1)) for grown in growns
    ]
    large = [nt_dot(jnp.concatenate(pair, axis=0), m) for pair, m in zip(pairs, tops)]
    tiny = [nt_dot(pair[0], m) for pair, m in zip(pairs, rests)]
    halves = []
    for x, y in zip(large, tiny):
        back = x[:32] + x[32:] + y
        a_r, b_r, a_i, b_i = back[:16, :128], back[16:, :128], back[:16, 128:], back[16:, 128:]
        back = jnp.concatenate([a_r + b_i, a_r - b_i, a_i - b_r, a_i + b_r], axis=0)
        halves.append(jnp.concatenate(split(back), axis=1))
    parts = [nn_dot(k, half) for k, half in zip(lefts, halves)]
    return [(part[:, :128] + part[:, 128:]).astype(BF).reshape(2, 32, 128) for part in parts]


def block_kernel(order_ref, pos_ref, plane_ref, *refs):
    obs_ref, uv_ref, wgt_ref, tile_ref, left_ref, leftt_ref, right_ref = refs[:7]
    res_ref, out_ref, u_tab, v_tab, prod, grown, coef, vis, seen_buf, seen_sem = refs[-10:]
    width = 32
    step = pl.program_id(0)
    now = lax.rem(step, 2)

    def fetch(turn, side):
        for b in range(STEP):
            pltpu.make_async_copy(
                obs_ref.at[order_ref[turn * STEP + b]], seen_buf.at[side, b], seen_sem.at[side]
            ).start()

    @pl.when(step == 0)
    def _():
        fetch(0, 0)

    @pl.when(step + 1 < pl.num_programs(0))
    def _():
        fetch(step + 1, 1 - now)

    pltpu.make_async_copy(obs_ref.at[pl.ds(0, STEP)], seen_buf.at[now], seen_sem.at[now]).wait()
    tables(uv_ref, u_tab, v_tab, width)
    sign = jnp.where(lax.broadcasted_iota(jnp.int32, (8, CHUNK), 0) < 4, -1.0, 1.0).astype(F32)

    def matrices_of(blocks, own):
        planes = [plane_ref[step * STEP + b] for b in blocks]
        return (
            [own[plane] for plane in planes],
            [right_ref[plane, 0] for plane in planes],
            [right_ref[plane, 1] for plane in planes],
        )

    def first(blocks):
        tiles = [tile_ref[pos_ref[step * STEP + b]] for b in blocks]
        for b, found in zip(blocks, forward(tiles, *matrices_of(blocks, left_ref))):
            for r in range(4):
                coef[b, 32 * r:32 * r + 32, :] = found[:, 64 * r:64 * r + 64]

    def products(b):
        for start in range(0, 1024, CHUNK):
            lanes = slice(start, start + CHUNK)
            table = column(u_tab, b, start)
            for r in range(4):
                row = row_of(v_tab, r, b, start, width)
                prod[b, width * r:width * r + width, lanes] = (table * row).astype(BF)

    def middle(b):
        for start in range(0, 1024, CHUNK):
            lanes = slice(start, start + CHUNK)
            spread = tn_dot(coef[b], prod[b, :, lanes])
            rows = [row_of(v_tab, 4 + g, b, start, 8) for g in range(8)]
            total = spread[0:8] * rows[0]
            for g in range(1, 8):
                total = total + spread[8 * g:8 * g + 8] * rows[g]
            phase_r, phase_i = row_of(v_tab, 12, b, start, 8), row_of(v_tab, 13, b, start, 8) * sign
            total = total * phase_r + swap_parts(total) * phase_i
            seen = jnp.concatenate([seen_buf[now, b, 0, :, lanes], seen_buf[now, b, 1, :, lanes]], axis=0)
            resid = seen - total
            res_ref[b, :, lanes] = resid
            scaled = resid * jnp.broadcast_to(wgt_ref[b:b + 1, lanes], (8, CHUNK))
            turned = scaled * phase_r - swap_parts(scaled) * phase_i
            for g in range(0, 8, 2):
                pair = jnp.concatenate([turned * rows[g], turned * rows[g + 1]], axis=0)
                vis[b, 8 * g:8 * g + 16, lanes] = pair.astype(BF)
        grown[b] = nt_dot(prod[b], vis[b])

    def last(blocks):
        done = backward([grown[b] for b in blocks], *matrices_of(blocks, leftt_ref))
        for b, part in zip(blocks, done):
            out_ref[pos_ref[step * STEP + b]] = part

    first(list(range(STEP)))
    for b in range(STEP):
        products(b)
        middle(b)
    last(list(range(STEP)))


def plane_matrices(w_kernels):
    planes, _, width, _ = w_kernels.shape
    half = width // 2
    turned = jnp.concatenate([w_kernels[:, :, half:], w_kernels[:, :, half - 1::-1]], axis=2)
    kr, ki = turned[:, 0], turned[:, 1]
    left = jnp.concatenate([jnp.concatenate([kr, -ki], axis=2), jnp.concatenate([ki, kr], axis=2)], axis=1)
    mix = np.zeros((4, 8, width), np.complex64)
    for r in range(4):
        for g in range(8):
            for s1 in (1, -1):
                for s3 in (1, -1):
                    i, n = r % 2, g % 4
                    m1 = 4 + n if s1 > 0 else 3 - n
                    m2 = 2 + i if s3 > 0 else 1 - i
                    mix[r, g, 4 * m1 + m2] = (1j * s3 if r >= 2 else 1) * (1j * s1 if g >= 4 else 1)
    spread = np.zeros((2, width, 2, 4, 8, 2, 4), np.float32)
    for into in range(2):
        for outof in range(2):
            for src in range(2):
                unit = 1j if src else 1
                factor = mix * unit
                if into == 0 and outof == 0:
                    value = factor.real
                elif into == 0 and outof == 1:
                    value = factor.imag
                elif into == 1 and outof == 0:
                    value = -factor.imag
                else:
                    value = factor.real
                spread[src, :, into, :, :, outof, :] = value.transpose(2, 0, 1)[:, :, :, None]
    spread = spread.reshape(2, width, 512)
    grid = jnp.einsum("zcmk,cmq->zkq", w_kernels, jnp.asarray(spread, BF), preferred_element_type=F32)
    grid = grid * (1.0 / width)
    top = lax.reduce_precision(grid, 8, 7)
    grid = jnp.stack([top.astype(BF), (grid - top).astype(BF)], axis=1)
    grid = grid.reshape(planes, 2, width, 2, 256).transpose(0, 1, 3, 2, 4)
    pol = np.arange(256) % 4
    mask = (pol[None, :] == np.arange(4)[:, None])[None, None, None, :, None, :]
    right = jnp.where(jnp.asarray(mask), grid[:, :, :, None, :, :], jnp.zeros((), BF))
    right = right.reshape(planes, 2, 256, 256)
    return left, left.transpose(0, 2, 1), right


def degrid_grid(phase, order, position, planes, vis_obs, uv_coords, vis_weight, arrived, matrices, residual):
    blocks = vis_obs.shape[0]
    count = order.shape[0]
    left, leftt, right = matrices

    def whole(array):
        zeros = (0,) * array.ndim
        return pl.BlockSpec(array.shape, lambda i, *_: zeros, pipeline_mode=pl.Buffered(1))

    steps = count // STEP
    first = phase * steps
    operands = [vis_obs, uv_coords, vis_weight, arrived, left, leftt, right]
    in_specs = [
        pl.BlockSpec(memory_space=pl.ANY),
        pl.BlockSpec((2, STEP, 1024), lambda i, *_: (0, i + first, 0)),
        pl.BlockSpec((STEP, 1024), lambda i, *_: (i + first, 0)),
        whole(arrived),
        whole(left),
        whole(leftt),
        whole(right),
    ]
    aliases = {}
    if residual is not None:
        operands.append(residual)
        in_specs.append(pl.BlockSpec(memory_space=pl.ANY))
        aliases = {3 + len(operands) - 1: 0}
    return pl.pallas_call(
        block_kernel,
        grid_spec=pltpu.PrefetchScalarGridSpec(
            num_scalar_prefetch=3,
            grid=(steps,),
            in_specs=in_specs,
            out_specs=[
                pl.BlockSpec((STEP, 8, 1024), lambda i, *_: (i + first, 0, 0)),
                whole(arrived),
            ],
            scratch_shapes=[
                pltpu.VMEM((8, 32 * STEP, 128), F32),
                pltpu.VMEM((8, 16 * STEP, 128), F32),
                pltpu.VMEM((STEP, 128, 1024), BF),
                pltpu.VMEM((STEP, 128, 64), F32),
                pltpu.VMEM((STEP, 128, 64), BF),
                pltpu.VMEM((STEP, 64, 1024), BF),
                pltpu.VMEM((2, STEP, 2, 4, 1024), F32),
                pltpu.SemaphoreType.DMA((2,)),
            ],
        ),
        out_shape=[
            jax.ShapeDtypeStruct((blocks, 8, 1024), F32),
            jax.ShapeDtypeStruct(arrived.shape, BF),
        ],
        input_output_aliases=aliases,
        compiler_params=pltpu.CompilerParams(vmem_limit_bytes=63 << 20),
        cost_estimate=pl.CostEstimate(flops=count * 80_000_000, bytes_accessed=count * 120_000, transcendentals=0),
        name=f"degrid_grid_{phase}",
    )(order, position, planes, *operands)


def sum_kernel(slot_ref, part_ref, start_ref, out_ref):
    step = pl.program_id(0)
    count = part_ref.shape[0]

    @pl.when(step == 0)
    def _():
        out_ref[...] = start_ref[...]

    def add(i, carry):
        slot = slot_ref[step * count + i]
        part = jnp.where(slot >= 0, part_ref[i].astype(F32), 0.0)
        row = jnp.maximum(slot, 0)
        out_ref[row] = out_ref[row] + part
        return carry

    lax.fori_loop(0, count, add, 0, unroll=8)


def sum_slots(slots, parts, start):
    steps = 2
    count = parts.shape[0] // steps
    shape = parts.shape[1:]

    def whole():
        return pl.BlockSpec(start.shape, lambda i, *_: (0, 0, 0, 0), pipeline_mode=pl.Buffered(1))

    return pl.pallas_call(
        sum_kernel,
        grid_spec=pltpu.PrefetchScalarGridSpec(
            num_scalar_prefetch=1,
            grid=(steps,),
            in_specs=[pl.BlockSpec((count,) + shape, lambda i, *_: (i, 0, 0, 0)), whole()],
            out_specs=whole(),
        ),
        out_shape=jax.ShapeDtypeStruct(start.shape, F32),
        compiler_params=pltpu.CompilerParams(vmem_limit_bytes=63 << 20),
        cost_estimate=pl.CostEstimate(flops=4_000_000, bytes_accessed=6_000_000, transcendentals=0),
        name="sum_slots",
    )(slots, parts, start)


def ask_kernel(target_ref, slot_ref, plane_ref, weight_ref, sorted_ref, ready, held, send_sem, recv_sem):
    blocks = target_ref.shape[1]
    facets, size = lax.axis_size("facet"), lax.axis_size("vis")
    groups = facets * size
    me = lax.axis_index("facet") * size + lax.axis_index("vis")
    barrier = pltpu.get_barrier_semaphore()

    def device(turn):
        peer = lax.rem(me + turn, groups)
        return peer, (peer // size, lax.rem(peer, size))

    def greet(turn):
        pl.semaphore_signal(barrier, inc=1, device_id=device(turn)[1], device_id_type=pl.DeviceIdType.MESH)

    def every(action):
        rounds = (groups - 1) // 7

        def some(i, carry):
            for j in range(1, 8):
                action(i * 7 + j)
            return carry

        lax.fori_loop(0, rounds, some, 0)
        for turn in range(rounds * 7 + 1, groups):
            action(turn)

    every(greet)

    square = (blocks, blocks)
    down = lax.broadcasted_iota(jnp.int32, square, 0)
    across = lax.broadcasted_iota(jnp.int32, square, 1)
    one, zero = jnp.ones(square, F32), jnp.zeros(square, F32)
    before = jnp.where(down < across, one, zero)
    equal = jnp.where(down == across, one, zero)

    def turned(row):
        return jnp.sum(equal * row, axis=1, keepdims=True)

    target_r, slot_r = target_ref[...].astype(F32), slot_ref[...].astype(F32)
    target_c, plane_c = turned(target_r), turned(plane_ref[...].astype(F32))
    same = jnp.where(jnp.abs(target_c - target_r) < 0.5, one, zero)
    rank = jnp.sum(same * before, axis=0, keepdims=True)
    double_r = jnp.where(jnp.sum(same, axis=0, keepdims=True) > 1.5, 1.0, 0.0)
    single_c = jnp.where(jnp.sum(same, axis=1, keepdims=True) > 1.5, 0.0, 1.0)
    ahead = jnp.sum(before * single_c, axis=0, keepdims=True)
    spare = 0.5 * blocks - 0.5 * jnp.sum(double_r, axis=1, keepdims=True)
    phase_r = double_r * rank + (1.0 - double_r) * jnp.where(ahead > spare - 0.5, 1.0, 0.0)
    asked = []
    for turn in range(2):
        mine = (jnp.abs(down.astype(F32) - target_r) < 0.5) & (jnp.abs(phase_r - turn) < 0.5)
        asked.append(jnp.max(jnp.where(mine, slot_r, -1.0), axis=1, keepdims=True))
    weight = jnp.sum(jnp.sum(weight_ref[...], axis=0, keepdims=True), axis=1, keepdims=True)
    ready[...] = jnp.where(across == 0, asked[0], jnp.where(across == 1, asked[1], weight))

    phase_c = turned(phase_r)
    alike = jnp.where(jnp.abs(phase_c - phase_r) < 0.5, one, zero)
    place_r = phase_r * (0.5 * blocks) + jnp.sum(before * alike, axis=0, keepdims=True)
    place_c = turned(place_r)
    at = jnp.where(jnp.abs(place_c - across.astype(F32)) < 0.5, one, zero)
    rows = [
        place_r,
        jnp.sum(at * down.astype(F32), axis=0, keepdims=True),
        jnp.sum(at * target_c, axis=0, keepdims=True),
        jnp.sum(at * plane_c, axis=0, keepdims=True),
    ]
    pl.semaphore_wait(barrier, groups - 1)

    def push(turn):
        peer, where = device(turn)
        pltpu.make_async_remote_copy(
            src_ref=ready.at[pl.ds(peer, 1)],
            dst_ref=held.at[pl.ds(me, 1)],
            send_sem=send_sem,
            recv_sem=recv_sem,
            device_id=where,
            device_id_type=pl.DeviceIdType.MESH,
        ).start()

    every(push)
    everything = pltpu.make_async_remote_copy(
        src_ref=ready.at[pl.ds(0, groups - 1)],
        dst_ref=held.at[pl.ds(0, groups - 1)],
        send_sem=send_sem,
        recv_sem=recv_sem,
        device_id=device(1)[1],
        device_id_type=pl.DeviceIdType.MESH,
    )
    everything.wait_send()
    everything.wait_recv()
    message = jnp.where(down == me, ready[...], held[...])
    for column in range(2):
        rows.append(jnp.sum(equal * message[:, column:column + 1], axis=0, keepdims=True))
    total = jnp.sum(message[:, 2:3], axis=0, keepdims=True)
    rows.append(jnp.broadcast_to(total, rows[0].shape))
    rows.append(rows[0])
    sorted_ref[...] = jnp.concatenate(rows, axis=0)


def ask(block_group, tile_slot, w_plane, vis_weight):
    blocks = tile_slot.shape[0]
    groups = lax.axis_size(AXES)
    rows = [array.reshape(1, blocks) for array in (block_group, tile_slot, w_plane)]
    return pl.pallas_call(
        ask_kernel,
        in_specs=[pl.BlockSpec(memory_space=pltpu.VMEM)] * 4,
        out_specs=pl.BlockSpec(memory_space=pltpu.VMEM),
        out_shape=jax.ShapeDtypeStruct((8, blocks), F32),
        scratch_shapes=[
            pltpu.VMEM((groups, 128), F32),
            pltpu.VMEM((groups, 128), F32),
            pltpu.SemaphoreType.DMA,
            pltpu.SemaphoreType.DMA,
        ],
        compiler_params=pltpu.CompilerParams(collective_id=0, has_side_effects=True),
        name="ask",
    )(*rows, vis_weight)


def shards(vis_obs, uv_coords, vis_weight, block_group, tile_slot, w_plane, model_tiles, w_kernels):
    blocks, nvis = vis_weight.shape
    groups = lax.axis_size(AXES)
    half = blocks // 2
    told = ask(block_group, tile_slot, w_plane, vis_weight)
    scale = (blocks * groups * nvis) / told[6, 0]
    place, order, position, planes = [told[row].astype(jnp.int32) for row in range(4)]
    requested = [told[row].astype(jnp.int32) for row in (4, 5)]

    def exchange(array):
        return lax.all_to_all(array, AXES, split_axis=0, concat_axis=0, tiled=True)

    chosen = [
        jnp.take(model_tiles, jnp.maximum(requested[turn], 0), axis=0, mode="clip")
        for turn in range(2)
    ]
    arrived = [exchange(chosen[0])]
    uv_sorted = jnp.take(uv_coords.transpose(1, 0, 2), order, axis=1, mode="clip")
    weight_sorted = jnp.take(vis_weight, order, axis=0, mode="clip") * scale
    matrices = plane_matrices(w_kernels)
    indices = [[values[:half], values[half:]] for values in (order, position, planes)]
    late, matrices, uv_sorted, weight_sorted, indices = lax.optimization_barrier(
        (chosen[1], matrices, uv_sorted, weight_sorted, indices)
    )
    arrived.append(exchange(late))
    residual = None
    returned = []
    for turn in range(2):
        residual, outgoing = degrid_grid(
            turn, *[values[turn] for values in indices], vis_obs, uv_sorted, weight_sorted,
            arrived[turn], matrices, residual
        )
        returned.append(exchange(outgoing))
    residual = jnp.take(residual, place, axis=0, mode="clip").reshape(vis_obs.shape)
    partial = sum_slots(requested[0], returned[0], jnp.zeros(model_tiles.shape, F32))
    return residual, sum_slots(requested[1], returned[1], partial)


def solution(mesh):
    return jax.shard_map(
        shards,
        mesh=mesh,
        in_specs=(
            P(AXES, None, None, None),
            P(AXES, None, None),
            P(AXES, None),
            P(AXES, None),
            P(AXES),
            P(AXES),
            P(AXES, None, None, None),
            P(),
        ),
        out_specs=(P(AXES, None, None, None), P(AXES, None, None, None)),
        check_vma=False,
    )
```
